32 devices in a mesh: seq: 8 (over z, x), head: 4 (over y, core).
Axes of the slice: x: 2, y: 2, z: 4, core: 2. Of those that a mesh axis runs over, the one named last changes fastest.
Arguments:
- queries: bfloat16 [4096, 4096], P('seq', 'head'), may hold values from -360 to 360, as said below
- key_rows: bfloat16 [4096, 1024], P('seq', 'head'), may hold values from -6 to 6
- value_rows: bfloat16 [4096, 1024], P('seq', 'head'), may hold values from -6 to 6
- doc_lengths: int32 [8], replicated, may hold values from 1 to 1536, 4096 in all
Outputs:
- attn_out: bfloat16 [4096, 4096], P(('seq', 'head'))
The draws below stay inside these ranges and needn't reach their ends.
Inputs may be any that keep to these rules, and one draw needn't show every extreme that they name: `queries`: custom draw of bounded query entries. `doc_lengths`: the lengths sum to 4096; each is at most 1536.
All inputs are finite; a program needn't handle non-finite values.
Results may differ from the reference program's by a relative error of at most 0.0036.
Values may be sent and summed in bfloat16 or wider, within the bound.
A program may use at most 64 MiB of HBM per device.

```python
import math
import jax
import jax.numpy as jnp
import numpy as np
from jax import lax

H = 32
KVH = 8
HD = 128
TOK_DEV = 512
SPAN = 4
TOKENS = 4096
MAXDOC = 1536
NDOCS = 8
N_SEQ = 8


def draw_queries(key, part):
    base = jnp.clip(jax.random.normal(key, (TOKENS, H * HD), jnp.float32), -4.5, 4.5)
    return base.astype(jnp.bfloat16)


def block_scale(own_key, shape, pieces, low, high):
    gain, own = 1.0, jax.random.fold_in(own_key, 6)
    for position, parts in pieces:
        heights = jnp.exp(jax.random.uniform(jax.random.fold_in(own, position), (parts,), jnp.float32, low / len(pieces), high / len(pieces)))
        gain = gain * jnp.repeat(heights, shape[position] // parts).reshape([-1 if axis == position else 1 for axis in range(len(shape))])
    return gain


def split_up(count, total, limit, slope):
    portions = [(1 << 20) // math.isqrt(standing ** slope) + 1 for standing in range(2, count + 1)]
    rest, counts = total - limit - (count - 1), [1] * (count - 1)
    while rest > 0:
        free = [i for i in range(count - 1) if counts[i] < limit]
        whole, left = sum([portions[i] for i in free]), rest
        for i in free:
            extra = min(limit - counts[i], max(1, left * portions[i] // whole), rest)
            counts[i] = counts[i] + extra
            rest = rest - extra
    return np.array([limit] + counts)


def ragged(key, amount, total, limit, slope):
    if amount == 2:
        one = jax.random.randint(key, (), max(1, total - limit), min(limit, total - 1) + 1)
        return jnp.stack([one, total - one])
    lengths = jnp.asarray(split_up(amount, total, limit, slope), jnp.int32)
    couples = (amount - 1) // 2
    source_of, sink = lengths[1:1 + 2 * couples:2], lengths[2:2 + 2 * couples:2]
    room = jnp.minimum(source_of - 1, limit - sink)
    passed = jax.random.randint(jax.random.fold_in(key, 1), (couples,), 0, 1 << 20) % (room + 1)
    lengths = lengths.at[1:1 + 2 * couples:2].set(source_of - passed).at[2:2 + 2 * couples:2].set(sink + passed)
    return lengths[jax.random.permutation(jax.random.fold_in(key, 2), amount)]


def noise(stream_key, shape, deviation, limit, split=(), kind=jnp.bfloat16):
    result = jax.random.normal(stream_key, shape, jnp.float32) * deviation
    if len(split) > 0:
        result = block_scale(stream_key, shape, split, -0.22, 0.18) * result
    return jnp.clip(result, min=-limit, max=limit).astype(kind)


def setup_inputs(seed: int = 0) -> dict:
    streams_of = jax.random.split(jax.random.key(seed), 5)
    return {
        "queries": draw_queries(jax.random.fold_in(streams_of[4], 71), 0),
        "key_rows": noise(streams_of[1], (TOKENS, KVH * HD), 1.0, 6.0, ((0, 8), (1, 4))),
        "value_rows": noise(streams_of[2], (TOKENS, KVH * HD), 1.0, 6.0, ((0, 8), (1, 4))),
        "doc_lengths": ragged(streams_of[3], NDOCS, TOKENS, MAXDOC, 2).astype(jnp.int32),
    }


scaling = 0.08838834764831845


def doc_index(ends, positions):
    return jnp.sum((ends[None, :] <= positions[:, None]).astype(jnp.int32), axis=1)


def reference(queries, key_rows, value_rows, doc_lengths):
    ends = jnp.cumsum(doc_lengths).astype(jnp.int32)
    group = H // KVH
    width = SPAN * TOK_DEV
    margin = (SPAN - 1) * TOK_DEV
    key_padded = jnp.concatenate([jnp.zeros((margin, KVH * HD), key_rows.dtype), key_rows], 0)
    value_padded = jnp.concatenate([jnp.zeros((margin, KVH * HD), value_rows.dtype), value_rows], 0)

    def block(index):
        start = (index * TOK_DEV).astype(jnp.int32)
        query_block = lax.dynamic_slice_in_dim(queries, start, TOK_DEV, 0).astype(jnp.float32).reshape(TOK_DEV, KVH, group, HD)
        key_block = lax.dynamic_slice_in_dim(key_padded, start, width, 0).astype(jnp.float32).reshape(width, KVH, HD)
        value_block = lax.dynamic_slice_in_dim(value_padded, start, width, 0).astype(jnp.float32).reshape(width, KVH, HD)
        query_pos = start + jnp.arange(TOK_DEV, dtype=jnp.int32)
        key_pos = start - margin + jnp.arange(width, dtype=jnp.int32)
        allowed = (key_pos[None, :] >= 0) & (doc_index(ends, key_pos)[None, :] == doc_index(ends, query_pos)[:, None]) & (key_pos[None, :] <= query_pos[:, None])
        scores = jnp.einsum("qgjd,kgd->gjqk", query_block, key_block, precision=lax.Precision.HIGHEST) * scaling
        scores = jnp.where(allowed[None, None], scores, jnp.float32(-1e30))
        largest = jnp.max(scores, axis=-1, keepdims=True)
        weights = jnp.where(allowed[None, None], jnp.exp(scores - largest), jnp.float32(0.0))
        total = jnp.sum(weights, axis=-1)
        rounded = lax.optimization_barrier(weights.astype(jnp.bfloat16)).astype(jnp.float32)
        output = jnp.einsum("gjqk,kgd->qgjd", rounded, value_block, precision=lax.Precision.HIGHEST)
        output = output / jnp.transpose(total, (2, 0, 1))[:, :, :, None]
        return output.reshape(TOK_DEV, H * HD).astype(jnp.bfloat16)

    blocks = lax.map(block, jnp.arange(N_SEQ, dtype=jnp.int32))
    return blocks.reshape(TOKENS, H * HD)
```

```python
import functools
import math

import jax
import jax.numpy as jnp
from jax import lax
from jax.experimental import pallas as pl
from jax.experimental.pallas import tpu as pltpu
from jax.sharding import PartitionSpec as P

H = 32
KVH = 8
HD = 128
SPAN = 4
FAR = -1e30
PAIR = 2
PIECES = 2
NEAR_AT = (1, 2)
GROUP = H // KVH
EXP2_SCALE = 0.08838834764831845 * math.log2(math.e)
MESH = pl.DeviceIdType.MESH


def kernel(
    n_seq, n_head, doc_ref, q_hbm, k_hbm, v_hbm, out_ref,
    qbuf, kbuf, vbuf, qdoc, kdoc, near_w, far_w, peak, fade, obuf,
    load_sem, send_sem, recv_sem, out_send, out_recv, own_sem,
):
    b = lax.axis_index("seq")
    h = lax.axis_index("head")
    tokens = q_hbm.shape[0]
    groups = k_hbm.shape[1] // HD
    tile = tokens // n_head
    width = GROUP * HD
    window = SPAN * tokens
    reach = (SPAN - 1) * tokens
    own = SPAN - 1
    even = b % 2 == 0
    odd = b % 2 == 1
    bufs = (kbuf, vbuf)
    K, V = 0, 1

    loads = {}
    for g in range(groups):
        for a, source in enumerate((k_hbm, v_hbm)):
            loads[g, a] = pltpu.make_async_copy(
                source.at[:, pl.ds(g * HD, HD)],
                bufs[a].at[g, pl.ds(reach, tokens), :],
                load_sem.at[g, a],
            )
    for load in loads.values():
        load.start()
    q_load = pltpu.make_async_copy(q_hbm, qbuf, load_sem.at[groups, 0])
    q_load.start()

    barrier = pltpu.get_barrier_semaphore()
    partner = b + 1 - 2 * (b % 2)
    has_next = b + 2 < n_seq
    has_last = b >= 2
    has_far = b >= SPAN - 1

    def greet(seq, head):
        pl.semaphore_signal(
            barrier, inc=1, device_id={"seq": seq, "head": head}, device_id_type=MESH
        )

    greet(partner, h)
    for off in range(1, n_head):
        greet(b, (h + off) % n_head)
    for condition, seq in ((has_next, b + 2), (has_last, b - 2)):
        @pl.when(condition)
        def _():
            greet(seq, h)

    pl.semaphore_wait(
        barrier, n_head + jnp.where(has_next, 1, 0) + jnp.where(has_last, 1, 0)
    )

    size = tokens // PIECES

    def hop(kind, g, a, p, source, target, slot):
        return pltpu.make_async_remote_copy(
            src_ref=bufs[a].at[g, pl.ds(source * tokens + p * size, size), :],
            dst_ref=bufs[a].at[g, pl.ds(slot * tokens + p * size, size), :],
            send_sem=send_sem.at[kind, g, a, p],
            recv_sem=recv_sem.at[slot, g, a, p],
            device_id={"seq": target, "head": h},
            device_id_type=MESH,
        )

    routes = {
        0: (even, (K, V), own, b + 1, 2),
        1: (even & has_next, (K,), own, b + 2, 1),
        2: (even & has_last, (K,), 1, b + 1, 0),
        3: (even & has_last & has_next, (K, V), 2, b + 2, 0),
        4: (odd & has_next, (K, V), own, b + 2, 1),
        5: (odd & has_last, (K, V), 1, b - 1, 2),
        6: (odd & has_next, (V,), 2, b + 2, 0),
        7: (odd & has_far, (V,), 0, b - 1, 1),
    }
    slot_of = {0: 0, 1: 1, 2: 2, 3: 3, 4: 1, 5: 2, 6: 3, 7: 4}

    def route(kind, g, a, p):
        condition, _, source, target, slot = routes[kind]
        return condition, hop(slot_of[kind], g, a, p, source, target, slot)

    def send(kind, g, a, p):
        condition, copy = route(kind, g, a, p)

        @pl.when(condition)
        def _():
            copy.start()

    def send_all(kind, g, a):
        for p in range(PIECES):
            send(kind, g, a, p)

    def arrive(who, slot, g, a, p):
        held = (has_far, has_last, odd | has_last)[slot]

        @pl.when(who & held)
        def _():
            hop(0, g, a, p, own, partner, slot).wait_recv()

    def arrive_all(who, slot, g, a):
        for p in range(PIECES):
            arrive(who, slot, g, a, p)

    def relay(kind, g, a, p):
        who = even if kind < 4 else odd
        arrive(who, routes[kind][2], g, a, p)
        send(kind, g, a, p)

    loads[0, K].wait()
    for p in range(PIECES):
        send(0, 0, K, p)
        send(1, 0, K, p)
        send(4, 0, K, p)
    loads[0, V].wait()
    send_all(0, 0, V)
    send_all(4, 0, V)
    for g in range(1, groups):
        loads[g, K].wait()
        send_all(1, g, K)
        loads[g, V].wait()

    lane = lax.broadcasted_iota(jnp.int32, (1, HD), 1)
    low = jnp.full((1, HD), 1 << 30, jnp.int32)
    high = jnp.full((1, HD), 0, jnp.int32)
    end = jnp.int32(0)
    for d in range(doc_ref.shape[0]):
        start = end
        end = end + doc_ref[d]
        low = jnp.where(lane == d, start, low)
        high = jnp.where(lane == d, end, high)
    first = b * tokens

    def key_docs(i, _):
        rows = i * tile
        pos = first - reach + rows + lax.broadcasted_iota(jnp.int32, (tile, HD), 0)
        same = (pos >= low) & (pos < high)
        kdoc[pl.ds(rows, tile), :] = jnp.where(same, 0.0, FAR).astype(jnp.bfloat16)
        return 0

    lax.fori_loop(0, window // tile, key_docs, 0)

    def query_docs(i, _):
        rows = i * tile
        pos = first + rows + lax.broadcasted_iota(jnp.int32, (tile, HD), 0)
        same = (pos >= low) & (pos < high)
        qdoc[pl.ds(rows, tile), :] = jnp.where(same, 1.0, 0.0).astype(jnp.bfloat16)
        return 0

    lax.fori_loop(0, n_head, query_docs, 0)

    for slot in range(SPAN - 1):
        @pl.when(b < SPAN - 1 - slot)
        def _():
            for g in range(groups):
                for buf in bufs:
                    buf[g, slot * tokens:(slot + 1) * tokens, :] = jnp.zeros((tokens, HD), jnp.bfloat16)

    q_load.wait()

    near = tokens * (SPAN - 2) + tile
    far = tokens
    pairs = n_head // 2

    def tile_at(i):
        return (h // 2 + pairs - 1 - i // 2) % pairs * 2 + (h % 2 + 1 - i % 2) % 2

    def source_at(i):
        return (h // 2 + 1 + i // 2) % pairs * 2 + (h % 2 + 1 - i % 2) % 2

    def columns(g, head):
        return pl.ds(pl.multiple_of((head * groups + g) * width, width), width)

    def deliver(g, i, t):
        return pltpu.make_async_remote_copy(
            src_ref=obuf.at[g, t],
            dst_ref=out_ref.at[:, columns(g, h)],
            send_sem=out_send.at[g, i],
            recv_sem=out_recv.at[g, i],
            device_id={"seq": b, "head": t},
            device_id_type=MESH,
        )

    def receive(g, i):
        source = source_at(i)
        return pltpu.make_async_remote_copy(
            src_ref=obuf.at[g, 0],
            dst_ref=out_ref.at[:, columns(g, source)],
            send_sem=out_send.at[g, i],
            recv_sem=out_recv.at[g, i],
            device_id={"seq": b, "head": source},
            device_id_type=MESH,
        )

    def keep(g):
        return pltpu.make_async_copy(
            obuf.at[g, h], out_ref.at[:, columns(g, h)], own_sem.at[g]
        )

    below = lax.broadcasted_iota(jnp.int32, (tile, tile), 1) <= lax.broadcasted_iota(
        jnp.int32, (tile, tile), 0
    )
    rows_all = GROUP * tile

    def scores_of(g, t, start, size):
        rows = pl.ds(pl.multiple_of(t * tile, tile), tile)
        keys = pl.ds(pl.multiple_of(start, tile), size)
        marks = qdoc[rows, :]
        query_ext = jnp.concatenate([
            jnp.concatenate([qbuf[rows, column:column + HD], marks], 1)
            for column in ((g * GROUP + m) * HD for m in range(GROUP))
        ], 0)
        key_ext = jnp.concatenate([kbuf[g, keys, :], kdoc[keys, :]], 1)
        return lax.dot_general(
            query_ext, key_ext, (((1,), (1,)), ((), ())), preferred_element_type=jnp.float32
        )

    def weigh_near(g, t):
        scores = scores_of(g, t, t * tile + far, near)
        edge = jnp.where(jnp.concatenate([below] * GROUP, 0), scores[:, near - tile:], FAR)
        scores = jnp.concatenate([scores[:, :near - tile], edge], 1)
        largest = jnp.max(scores, axis=1, keepdims=True)
        near_w[t] = jnp.exp2((scores - largest) * EXP2_SCALE).astype(jnp.bfloat16)
        peak[t] = jnp.broadcast_to(largest, (rows_all, HD))

    def weigh_far(g, t):
        scores = scores_of(g, t, t * tile, far)
        before = peak[t]
        largest = jnp.maximum(jnp.max(scores, axis=1, keepdims=True), before)
        fade[t] = jnp.exp2((before - largest) * EXP2_SCALE)
        far_w[t] = jnp.exp2(
            (scores - jnp.concatenate([largest] * (far // HD), 1)) * EXP2_SCALE
        ).astype(jnp.bfloat16)

    def values_of(g, start, size):
        keys = pl.ds(pl.multiple_of(start, tile), size)
        return jnp.concatenate([vbuf[g, keys, :], jnp.ones((size, HD), jnp.bfloat16)], 1)

    def blend(g, t):
        near_v = values_of(g, t * tile + far, near)
        far_v = values_of(g, t * tile, far)
        for part in range(GROUP // PAIR):
            rows = slice(part * PAIR * tile, (part + 1) * PAIR * tile)
            faded = fade[t, rows, :]
            mixed = jnp.dot(near_w[t, rows, :], near_v, preferred_element_type=jnp.float32)
            mixed = mixed * jnp.concatenate([faded, faded], 1) + jnp.dot(
                far_w[t, rows, :], far_v, preferred_element_type=jnp.float32
            )
            result = (mixed[:, :HD] / mixed[:, HD:]).astype(jnp.bfloat16)
            for m in range(PAIR):
                column = (part * PAIR + m) * HD
                obuf[g, t, :, column:column + HD] = result[m * tile:(m + 1) * tile]

    for p in range(PIECES):
        relay(2, 0, K, p)
        relay(5, 0, K, p)
    for g in range(1, groups):
        for a in (K, V):
            send_all(0, g, a)
    arrive_all(odd, 2, 0, K)
    for p in range(PIECES):
        relay(3, 0, K, p)

    for g in range(groups):
        later = g + 1 < groups

        def near_step(i, _):
            weigh_near(g, tile_at(i))
            for p, when in enumerate(NEAR_AT):
                @pl.when(i == when)
                def _():
                    relay(5, g, V, p)
                    relay(6, g, V, p)
                    relay(3, g, V, p)
                    if later and p == PIECES - 1:
                        send_all(4, g + 1, K)
                        send_all(4, g + 1, V)
            return 0

        lax.fori_loop(0, n_head, near_step, 0)
        for p in range(PIECES):
            arrive(even | odd, 0, g, K, p)
            relay(7, g, V, p)

        def far_step(i, _):
            weigh_far(g, tile_at(i))
            return 0

        lax.fori_loop(0, n_head, far_step, 0)
        if later:
            for p in range(PIECES):
                relay(2, g + 1, K, p)
            relay(5, g + 1, K, 0)
        arrive_all(even, 1, g, V)
        arrive_all(even, 0, g, V)

        def blend_step(i, _):
            t = tile_at(i)
            blend(g, t)

            @pl.when(i < n_head - 1)
            def _():
                deliver(g, i, t).start()

            @pl.when(i == n_head - 1)
            def _():
                keep(g).start()

            if later:
                for p in range(PIECES):
                    @pl.when(i == 1 + p)
                    def _():
                        if p > 0:
                            relay(5, g + 1, K, p)
                        relay(3, g + 1, K, p)
            return 0

        lax.fori_loop(0, n_head, blend_step, 0)
        if later:
            arrive_all(odd, 2, g + 1, K)

    for kind, (condition, which, *_) in routes.items():
        @pl.when(condition)
        def _():
            for g in range(groups):
                for a in which:
                    for p in range(PIECES):
                        route(kind, g, a, p)[1].wait_send()
    for g in range(groups):
        keep(g).wait()
        for i in range(n_head - 1):
            deliver(g, i, tile_at(i)).wait_send()
            receive(g, i).wait_recv()


def per_device(n_seq, n_head, queries, key_rows, value_rows, doc_lengths):
    tokens = queries.shape[0]
    groups = key_rows.shape[1] // HD
    tile = tokens // n_head
    window = SPAN * tokens
    flops = 4 * tokens * (GROUP * groups) * window * HD
    return pl.pallas_call(
        functools.partial(kernel, n_seq, n_head),
        out_shape=pltpu.VMEM((tile, H * HD), jnp.bfloat16),
        in_specs=[pl.BlockSpec(memory_space=pltpu.SMEM)]
        + [pl.BlockSpec(memory_space=pl.ANY)] * 3,
        out_specs=pl.BlockSpec(memory_space=pl.ANY),
        scratch_shapes=[
            pltpu.VMEM((tokens, GROUP * groups * HD), jnp.bfloat16),
            pltpu.VMEM((groups, window, HD), jnp.bfloat16),
            pltpu.VMEM((groups, window, HD), jnp.bfloat16),
            pltpu.VMEM((tokens, HD), jnp.bfloat16),
            pltpu.VMEM((window, HD), jnp.bfloat16),
            pltpu.VMEM((n_head, GROUP * tile, tokens * (SPAN - 2) + tile), jnp.bfloat16),
            pltpu.VMEM((n_head, GROUP * tile, tokens), jnp.bfloat16),
            pltpu.VMEM((n_head, GROUP * tile, HD), jnp.float32),
            pltpu.VMEM((n_head, GROUP * tile, HD), jnp.float32),
            pltpu.VMEM((groups, n_head, tile, GROUP * HD), jnp.bfloat16),
            pltpu.SemaphoreType.DMA((groups + 1, 2)),
            pltpu.SemaphoreType.DMA((5, groups, 2, PIECES)),
            pltpu.SemaphoreType.DMA((SPAN - 1, groups, 2, PIECES)),
            pltpu.SemaphoreType.DMA((groups, n_head - 1)),
            pltpu.SemaphoreType.DMA((groups, n_head - 1)),
            pltpu.SemaphoreType.DMA((groups,)),
        ],
        compiler_params=pltpu.CompilerParams(
            collective_id=0, has_side_effects=True, vmem_limit_bytes=56 << 20
        ),
        cost_estimate=pl.CostEstimate(flops=flops, bytes_accessed=4 << 20, transcendentals=0),
    )(doc_lengths, queries, key_rows, value_rows)


def solution(mesh):
    body = functools.partial(per_device, mesh.shape["seq"], mesh.shape["head"])
    in_specs = (P("seq", "head"), P("seq", "head"), P("seq", "head"), P())
    out_specs = P(("seq", "head"), None)
    return jax.shard_map(body, mesh=mesh, in_specs=in_specs, out_specs=out_specs, check_vma=False)
```

```python
import functools
import math

import jax
import jax.numpy as jnp
from jax import lax
from jax.experimental import pallas as pl
from jax.experimental.pallas import tpu as pltpu
from jax.sharding import PartitionSpec as P

H = 32
KVH = 8
HD = 128
SPAN = 4
FAR = -1e30
PAIR = 2
PIECES = 4
KEYS, VALUES = 0, 1
ALL = (0, 1, 2, 3)
HIGH = ((0, 1, 2, 3), (3,))
LOW = ((), (0, 1, 2))
EVEN_PLAN = {
    ("near", 0): (("next", 0, KEYS, (0, 1, 2, 3)), ("next", 0, VALUES, (0, 2)), ("next", 2, KEYS, (3,)), ("next", 0, VALUES, (1,)), ("now", 3, VALUES, (0,)),),
    ("near", 1): (("now", 3, VALUES, (2,)),),
    ("near", 2): (("next", 2, KEYS, (0, 2)), ("now", 3, VALUES, (1,)),),
    ("near", 3): (("next", 2, KEYS, (1,)), ("now", 3, VALUES, (3,)),),
    ("far", 0): (("next", 3, KEYS, (0,)),),
    ("far", 1): (("next", 2, VALUES, (3,)), ("next", 0, VALUES, (3,)),),
    ("far", 2): (("next", 3, KEYS, (2,)),),
    ("blend", 3): (("next", 3, KEYS, (1, 3)),),
}
ODD_PLAN = {
    ("near", 0): (("next", 4, KEYS, (2, 0)), ("now", 6, VALUES, (0,)), ("now", 5, VALUES, (2,)),),
    ("near", 1): (("now", 6, VALUES, (1,)), ("now", 5, VALUES, (1, 3)),),
    ("near", 2): (("next", 5, KEYS, (2,)), ("now", 6, VALUES, (2,)),),
    ("near", 3): (("next", 4, KEYS, (3,)), ("next", 5, KEYS, (0,)), ("next", 4, VALUES, (2,)), ("now", 7, VALUES, (0,)),),
    ("far", 0): (("next", 4, KEYS, (1,)), ("now", 7, VALUES, (1,)),),
    ("far", 1): (("next", 4, VALUES, (0, 3)), ("now", 7, VALUES, (2,)),),
    ("far", 3): (("next", 5, KEYS, (3,)),),
    ("blend", 0): (("next", 4, VALUES, (1,)), ("next", 5, KEYS, (1,)),),
    ("blend", 2): (("next", 5, VALUES, (0,)),),
}
EVEN_START = (
    (0, KEYS, (2, 0, 1, 3)),
    (0, VALUES, (0, 1, 2)),
    (2, KEYS, (2, 1, 0, 3)),
    (0, VALUES, (3,)),
    (3, KEYS, (3,)),
    (2, VALUES, (3,)),
    (3, KEYS, (1, 2, 0)),
)
ODD_START = (
    (4, KEYS, (0, 1, 2, 3)),
    (4, VALUES, (0, 3, 2, 1)),
    (5, KEYS, (0, 1, 2, 3)),
    (5, VALUES, (0,)),
)
GROUP = H // KVH
EXP2_SCALE = 0.08838834764831845 * math.log2(math.e)
MESH = pl.DeviceIdType.MESH


def kernel(
    n_seq, n_head, doc_ref, q_hbm, k_hbm, v_hbm, out_ref,
    qbuf, kbuf, vbuf, qdoc, kdoc, near_w, far_w, peak, fade, obuf,
    load_sem, send_sem, recv_sem, out_send, out_recv, own_sem,
):
    b = lax.axis_index("seq")
    h = lax.axis_index("head")
    tokens = q_hbm.shape[0]
    groups = k_hbm.shape[1] // HD
    tile = tokens // n_head
    width = GROUP * HD
    window = SPAN * tokens
    reach = (SPAN - 1) * tokens
    own = SPAN - 1
    even = b % 2 == 0
    odd = b % 2 == 1
    bufs = (kbuf, vbuf)
    K, V = KEYS, VALUES

    loads = {}
    for g in range(groups):
        for a, source in enumerate((k_hbm, v_hbm)):
            loads[g, a] = pltpu.make_async_copy(
                source.at[:, pl.ds(g * HD, HD)],
                bufs[a].at[g, pl.ds(reach, tokens), :],
                load_sem.at[g, a],
            )
    for load in loads.values():
        load.start()
    q_load = pltpu.make_async_copy(q_hbm, qbuf, load_sem.at[groups, 0])
    q_load.start()

    barrier = pltpu.get_barrier_semaphore()
    partner = b + 1 - 2 * (b % 2)
    has_next = b + 2 < n_seq
    has_last = b >= 2
    has_far = b >= SPAN - 1

    def greet(seq, head):
        pl.semaphore_signal(
            barrier, inc=1, device_id={"seq": seq, "head": head}, device_id_type=MESH
        )

    greet(partner, h)
    for off in range(1, n_head):
        greet(b, (h + off) % n_head)
    for condition, seq in ((has_next, b + 2), (has_last, b - 2)):
        @pl.when(condition)
        def _():
            greet(seq, h)

    pl.semaphore_wait(
        barrier, n_head + jnp.where(has_next, 1, 0) + jnp.where(has_last, 1, 0)
    )

    size = tokens // PIECES

    def hop(kind, g, a, p, source, target, slot):
        return pltpu.make_async_remote_copy(
            src_ref=bufs[a].at[g, pl.ds(source * tokens + p * size, size), :],
            dst_ref=bufs[a].at[g, pl.ds(slot * tokens + p * size, size), :],
            send_sem=send_sem.at[kind, g, a, p],
            recv_sem=recv_sem.at[slot, g, a, p],
            device_id={"seq": target, "head": h},
            device_id_type=MESH,
        )

    routes = {
        0: (even, (ALL, ALL), own, b + 1, 2),
        1: (even & has_next, HIGH, own, b + 2, 1),
        2: (even & has_last, HIGH, 1, b + 1, 0),
        3: (even & has_last & has_next, (ALL, ALL), 2, b + 2, 0),
        4: (odd & has_next, (ALL, ALL), own, b + 2, 1),
        5: (odd & has_last, (ALL, ALL), 1, b - 1, 2),
        6: (odd & has_next, LOW, 2, b + 2, 0),
        7: (odd & has_far, LOW, 0, b - 1, 1),
    }
    slot_of = {0: 0, 1: 1, 2: 2, 3: 3, 4: 1, 5: 2, 6: 3, 7: 4}

    def route(kind, g, a, p):
        condition, _, source, target, slot = routes[kind]
        return condition, hop(slot_of[kind], g, a, p, source, target, slot)

    def send(kind, g, a, p):
        condition, copy = route(kind, g, a, p)

        @pl.when(condition)
        def _():
            copy.start()

    def arrive(who, slot, g, a, p):
        held = (has_far, has_last, odd | has_last)[slot]

        @pl.when(who & held)
        def _():
            hop(0, g, a, p, own, partner, slot).wait_recv()

    def wait_for(who, slot, g, a, pieces):
        for p in pieces:
            arrive(who, slot, g, a, p)

    def relay(kind, g, a, pieces):
        who = even if kind < 4 else odd
        source = routes[kind][2]
        for p in pieces:
            if source != own:
                arrive(who, source, g, a, p)
            send(kind, g, a, p)

    def follow(phase, i, g):
        for parity, plan in ((even, EVEN_PLAN), (odd, ODD_PLAN)):
            for (name, step), events in plan.items():
                todo = [
                    (kind, g + (when == "next"), a, pieces)
                    for when, kind, a, pieces in events
                    if g + (when == "next") < groups
                ]
                if name == phase and todo:
                    @pl.when(parity & (i == min(step, n_head - 1)))
                    def _():
                        for event in todo:
                            relay(*event)

    starts = []
    for parity, events in ((even, EVEN_START), (odd, ODD_START)):
        count = 0
        while routes[events[count][0]][2] == own:
            count += 1
        starts.append((parity, events[:count], events[count:]))
    for g in range(groups):
        for a in (K, V):
            loads[g, a].wait()
            if g == 0:
                for _, events, _ in starts:
                    for kind, array, pieces in events:
                        if array == a:
                            relay(kind, g, a, pieces)
            relay(1, g, a, HIGH[a])

    lane = lax.broadcasted_iota(jnp.int32, (1, HD), 1)
    low = jnp.full((1, HD), 1 << 30, jnp.int32)
    high = jnp.full((1, HD), 0, jnp.int32)
    end = jnp.int32(0)
    for d in range(doc_ref.shape[0]):
        start = end
        end = end + doc_ref[d]
        low = jnp.where(lane == d, start, low)
        high = jnp.where(lane == d, end, high)
    first = b * tokens

    def key_docs(i, _):
        rows = i * tile
        pos = first - reach + rows + lax.broadcasted_iota(jnp.int32, (tile, HD), 0)
        same = (pos >= low) & (pos < high)
        kdoc[pl.ds(rows, tile), :] = jnp.where(same, 0.0, FAR).astype(jnp.bfloat16)
        return 0

    lax.fori_loop(0, window // tile, key_docs, 0)

    def query_docs(i, _):
        rows = i * tile
        pos = first + rows + lax.broadcasted_iota(jnp.int32, (tile, HD), 0)
        same = (pos >= low) & (pos < high)
        qdoc[pl.ds(rows, tile), :] = jnp.where(same, 1.0, 0.0).astype(jnp.bfloat16)
        return 0

    lax.fori_loop(0, n_head, query_docs, 0)

    for slot in range(SPAN - 1):
        @pl.when(b < SPAN - 1 - slot)
        def _():
            for g in range(groups):
                for buf in bufs:
                    buf[g, slot * tokens:(slot + 1) * tokens, :] = jnp.zeros((tokens, HD), jnp.bfloat16)

    q_load.wait()

    near = tokens * (SPAN - 2) + tile
    far = tokens
    pairs = n_head // 2

    def tile_at(i):
        return (h // 2 + pairs - 1 - i // 2) % pairs * 2 + (h % 2 + 1 - i % 2) % 2

    def source_at(i):
        return (h // 2 + 1 + i // 2) % pairs * 2 + (h % 2 + 1 - i % 2) % 2

    def columns(g, head):
        return pl.ds(pl.multiple_of((head * groups + g) * width, width), width)

    def deliver(g, i, t):
        return pltpu.make_async_remote_copy(
            src_ref=obuf.at[g, t],
            dst_ref=out_ref.at[:, columns(g, h)],
            send_sem=out_send.at[g, i],
            recv_sem=out_recv.at[g, i],
            device_id={"seq": b, "head": t},
            device_id_type=MESH,
        )

    def receive(g, i):
        source = source_at(i)
        return pltpu.make_async_remote_copy(
            src_ref=obuf.at[g, 0],
            dst_ref=out_ref.at[:, columns(g, source)],
            send_sem=out_send.at[g, i],
            recv_sem=out_recv.at[g, i],
            device_id={"seq": b, "head": source},
            device_id_type=MESH,
        )

    def keep(g):
        return pltpu.make_async_copy(
            obuf.at[g, h], out_ref.at[:, columns(g, h)], own_sem.at[g]
        )

    below = lax.broadcasted_iota(jnp.int32, (tile, tile), 1) <= lax.broadcasted_iota(
        jnp.int32, (tile, tile), 0
    )
    rows_all = GROUP * tile

    def scores_of(g, t, start, size):
        rows = pl.ds(pl.multiple_of(t * tile, tile), tile)
        keys = pl.ds(pl.multiple_of(start, tile), size)
        marks = qdoc[rows, :]
        query_ext = jnp.concatenate([
            jnp.concatenate([qbuf[rows, column:column + HD], marks], 1)
            for column in ((g * GROUP + m) * HD for m in range(GROUP))
        ], 0)
        key_ext = jnp.concatenate([kbuf[g, keys, :], kdoc[keys, :]], 1)
        return lax.dot_general(
            query_ext, key_ext, (((1,), (1,)), ((), ())), preferred_element_type=jnp.float32
        )

    def weigh_near(g, t):
        scores = scores_of(g, t, t * tile + far, near)
        edge = jnp.where(jnp.concatenate([below] * GROUP, 0), scores[:, near - tile:], FAR)
        scores = jnp.concatenate([scores[:, :near - tile], edge], 1)
        largest = jnp.max(scores, axis=1, keepdims=True)
        near_w[t] = jnp.exp2((scores - largest) * EXP2_SCALE).astype(jnp.bfloat16)
        peak[t] = jnp.broadcast_to(largest, (rows_all, HD))

    def weigh_far(g, t):
        scores = scores_of(g, t, t * tile, far)
        before = peak[t]
        largest = jnp.maximum(jnp.max(scores, axis=1, keepdims=True), before)
        fade[t] = jnp.exp2((before - largest) * EXP2_SCALE)
        far_w[t] = jnp.exp2(
            (scores - jnp.concatenate([largest] * (far // HD), 1)) * EXP2_SCALE
        ).astype(jnp.bfloat16)

    def values_of(g, start, size):
        keys = pl.ds(pl.multiple_of(start, tile), size)
        return jnp.concatenate([vbuf[g, keys, :], jnp.ones((size, HD), jnp.bfloat16)], 1)

    def blend(g, t):
        near_v = values_of(g, t * tile + far, near)
        far_v = values_of(g, t * tile, far)
        for part in range(GROUP // PAIR):
            rows = slice(part * PAIR * tile, (part + 1) * PAIR * tile)
            faded = fade[t, rows, :]
            mixed = jnp.dot(near_w[t, rows, :], near_v, preferred_element_type=jnp.float32)
            mixed = mixed * jnp.concatenate([faded, faded], 1) + jnp.dot(
                far_w[t, rows, :], far_v, preferred_element_type=jnp.float32
            )
            result = (mixed[:, :HD] / mixed[:, HD:]).astype(jnp.bfloat16)
            for m in range(PAIR):
                column = (part * PAIR + m) * HD
                obuf[g, t, :, column:column + HD] = result[m * tile:(m + 1) * tile]

    for parity, _, events in starts:
        @pl.when(parity)
        def _():
            for kind, a, pieces in events:
                relay(kind, 0, a, pieces)

    for g in range(groups):
        wait_for(even, 1, g, K, LOW[K])
        wait_for(odd, 2, g, K, HIGH[K])

        def near_step(i, _):
            weigh_near(g, tile_at(i))
            follow("near", i, g)
            return 0

        lax.fori_loop(0, n_head, near_step, 0)
        wait_for(even, 0, g, K, ALL)
        wait_for(odd, 0, g, K, HIGH[K])

        def far_step(i, _):
            weigh_far(g, tile_at(i))
            follow("far", i, g)
            return 0

        lax.fori_loop(0, n_head, far_step, 0)
        wait_for(even, 1, g, V, LOW[V])
        wait_for(odd, 2, g, V, HIGH[V])
        wait_for(even, 0, g, V, ALL)
        wait_for(odd, 0, g, V, HIGH[V])

        def blend_step(i, _):
            t = tile_at(i)
            blend(g, t)

            @pl.when(i < n_head - 1)
            def _():
                deliver(g, i, t).start()

            @pl.when(i == n_head - 1)
            def _():
                keep(g).start()

            follow("blend", i, g)
            return 0

        lax.fori_loop(0, n_head, blend_step, 0)

    for kind, (condition, pieces, *_) in routes.items():
        @pl.when(condition)
        def _():
            for g in range(groups):
                for a in (K, V):
                    for p in pieces[a]:
                        route(kind, g, a, p)[1].wait_send()
    for g in range(groups):
        keep(g).wait()
        for i in range(n_head - 1):
            deliver(g, i, tile_at(i)).wait_send()
            receive(g, i).wait_recv()


def per_device(n_seq, n_head, queries, key_rows, value_rows, doc_lengths):
    tokens = queries.shape[0]
    groups = key_rows.shape[1] // HD
    tile = tokens // n_head
    window = SPAN * tokens
    flops = 4 * tokens * (GROUP * groups) * window * HD
    return pl.pallas_call(
        functools.partial(kernel, n_seq, n_head),
        out_shape=pltpu.VMEM((tile, H * HD), jnp.bfloat16),
        in_specs=[pl.BlockSpec(memory_space=pltpu.SMEM)]
        + [pl.BlockSpec(memory_space=pl.ANY)] * 3,
        out_specs=pl.BlockSpec(memory_space=pl.ANY),
        scratch_shapes=[
            pltpu.VMEM((tokens, GROUP * groups * HD), jnp.bfloat16),
            pltpu.VMEM((groups, window, HD), jnp.bfloat16),
            pltpu.VMEM((groups, window, HD), jnp.bfloat16),
            pltpu.VMEM((tokens, HD), jnp.bfloat16),
            pltpu.VMEM((window, HD), jnp.bfloat16),
            pltpu.VMEM((n_head, GROUP * tile, tokens * (SPAN - 2) + tile), jnp.bfloat16),
            pltpu.VMEM((n_head, GROUP * tile, tokens), jnp.bfloat16),
            pltpu.VMEM((n_head, GROUP * tile, HD), jnp.float32),
            pltpu.VMEM((n_head, GROUP * tile, HD), jnp.float32),
            pltpu.VMEM((groups, n_head, tile, GROUP * HD), jnp.bfloat16),
            pltpu.SemaphoreType.DMA((groups + 1, 2)),
            pltpu.SemaphoreType.DMA((5, groups, 2, PIECES)),
            pltpu.SemaphoreType.DMA((SPAN - 1, groups, 2, PIECES)),
            pltpu.SemaphoreType.DMA((groups, n_head - 1)),
            pltpu.SemaphoreType.DMA((groups, n_head - 1)),
            pltpu.SemaphoreType.DMA((groups,)),
        ],
        compiler_params=pltpu.CompilerParams(
            collective_id=0, has_side_effects=True, vmem_limit_bytes=56 << 20
        ),
        cost_estimate=pl.CostEstimate(flops=flops, bytes_accessed=4 << 20, transcendentals=0),
    )(doc_lengths, queries, key_rows, value_rows)


def solution(mesh):
    body = functools.partial(per_device, mesh.shape["seq"], mesh.shape["head"])
    in_specs = (P("seq", "head"), P("seq", "head"), P("seq", "head"), P())
    out_specs = P(("seq", "head"), None)
    return jax.shard_map(body, mesh=mesh, in_specs=in_specs, out_specs=out_specs, check_vma=False)
```

```python
import functools
import math

import jax
import jax.numpy as jnp
from jax import lax
from jax.experimental import pallas as pl
from jax.experimental.pallas import tpu as pltpu
from jax.sharding import PartitionSpec as P

H = 32
KVH = 8
HD = 128
SPAN = 4
FAR = -1e30
PAIR = 2
PIECES = 4
KEYS, VALUES = 0, 1
ALL = (0, 1, 2, 3)
HIGH = ((0, 1, 2, 3), (3,))
LOW = ((), (0, 1, 2))
EVEN_PLAN = {
    ("near", 0): (("next", 0, KEYS, (0, 1, 2, 3)), ("now", 3, VALUES, (1,)),),
    ("near", 1): (("next", 0, VALUES, (0,)), ("now", 3, VALUES, (0,)),),
    ("near", 2): (("next", 0, VALUES, (1,)), ("now", 3, VALUES, (2, 3)),),
    ("far", 1): (("next", 0, VALUES, (2,)), ("next", 2, KEYS, (3, 0, 2, 1)),),
    ("far", 3): (("next", 0, VALUES, (3,)), ("next", 3, KEYS, (1,)),),
    ("blend", 0): (("next", 3, KEYS, (0,)),),
    ("blend", 1): (("next", 2, VALUES, (3,)), ("next", 3, KEYS, (2, 3)),),
}
ODD_PLAN = {
    ("near", 0): (("next", 4, KEYS, (1, 0)), ("now", 5, VALUES, (0, 2)), ("now", 6, VALUES, (0, 1)),),
    ("near", 1): (("now", 5, VALUES, (3,)), ("now", 6, VALUES, (2,)),),
    ("near", 2): (("next", 5, KEYS, (0,)), ("next", 4, KEYS, (2,)), ("next", 5, KEYS, (1,)), ("next", 4, KEYS, (3,)), ("now", 7, VALUES, (0,)),),
    ("near", 3): (("next", 4, VALUES, (1, 0, 2)), ("now", 7, VALUES, (1, 2)),),
    ("far", 1): (("next", 5, KEYS, (2,)),),
    ("far", 3): (("next", 5, KEYS, (3,)),),
    ("blend", 0): (("next", 4, VALUES, (3,)),),
    ("blend", 1): (("next", 5, VALUES, (1,)),),
}
EVEN_START = (
    (0, KEYS, (0, 2, 1, 3)),
    (0, VALUES, (0, 1, 2, 3)),
    (2, KEYS, (0, 2, 3, 1)),
    (2, VALUES, (3,)),
    (3, KEYS, (0, 2, 3, 1)),
)
ODD_START = (
    (4, KEYS, (0, 2, 3, 1)),
    (4, VALUES, (1,)),
    (5, KEYS, (0,)),
    (4, VALUES, (2, 0)),
    (5, KEYS, (2,)),
    (4, VALUES, (3,)),
    (5, KEYS, (3, 1)),
    (5, VALUES, (1,)),
)
GROUP = H // KVH
EXP2_SCALE = 0.08838834764831845 * math.log2(math.e)
MESH = pl.DeviceIdType.MESH


def kernel(
    n_seq, n_head, doc_ref, q_hbm, k_hbm, v_hbm, out_ref,
    qbuf, kbuf, vbuf, qdoc, kdoc, near_w, far_w, peak, fade, obuf,
    load_sem, send_sem, recv_sem, out_send, out_recv, own_sem,
):
    b = lax.axis_index("seq")
    h = lax.axis_index("head")
    tokens = q_hbm.shape[0]
    groups = k_hbm.shape[1] // HD
    tile = tokens // n_head
    width = GROUP * HD
    window = SPAN * tokens
    reach = (SPAN - 1) * tokens
    own = SPAN - 1
    even = b % 2 == 0
    odd = b % 2 == 1
    bufs = (kbuf, vbuf)
    K, V = KEYS, VALUES

    loads = {}
    for g in range(groups):
        for a, source in enumerate((k_hbm, v_hbm)):
            loads[g, a] = pltpu.make_async_copy(
                source.at[:, pl.ds(g * HD, HD)],
                bufs[a].at[g, pl.ds(reach, tokens), :],
                load_sem.at[g, a],
            )
    for load in loads.values():
        load.start()
    q_load = pltpu.make_async_copy(q_hbm, qbuf, load_sem.at[groups, 0])
    q_load.start()

    barrier = pltpu.get_barrier_semaphore()
    partner = b + 1 - 2 * (b % 2)
    has_next = b + 2 < n_seq
    has_last = b >= 2
    has_far = b >= SPAN - 1

    def greet(seq, head):
        pl.semaphore_signal(
            barrier, inc=1, device_id={"seq": seq, "head": head}, device_id_type=MESH
        )

    greet(partner, h)
    for off in range(1, n_head):
        greet(b, (h + off) % n_head)
    for condition, seq in ((has_next, b + 2), (has_last, b - 2)):
        @pl.when(condition)
        def _():
            greet(seq, h)

    pl.semaphore_wait(
        barrier, n_head + jnp.where(has_next, 1, 0) + jnp.where(has_last, 1, 0)
    )

    size = tokens // PIECES

    def hop(kind, g, a, p, source, target, slot):
        return pltpu.make_async_remote_copy(
            src_ref=bufs[a].at[g, pl.ds(source * tokens + p * size, size), :],
            dst_ref=bufs[a].at[g, pl.ds(slot * tokens + p * size, size), :],
            send_sem=send_sem.at[kind, g, a, p],
            recv_sem=recv_sem.at[slot, g, a, p],
            device_id={"seq": target, "head": h},
            device_id_type=MESH,
        )

    routes = {
        0: (even, (ALL, ALL), own, b + 1, 2),
        1: (even & has_next, HIGH, own, b + 2, 1),
        2: (even & has_last, HIGH, 1, b + 1, 0),
        3: (even & has_last & has_next, (ALL, ALL), 2, b + 2, 0),
        4: (odd & has_next, (ALL, ALL), own, b + 2, 1),
        5: (odd & has_last, (ALL, ALL), 1, b - 1, 2),
        6: (odd & has_next, LOW, 2, b + 2, 0),
        7: (odd & has_far, LOW, 0, b - 1, 1),
    }
    slot_of = {0: 0, 1: 1, 2: 2, 3: 3, 4: 1, 5: 2, 6: 3, 7: 4}

    def route(kind, g, a, p):
        condition, _, source, target, slot = routes[kind]
        return condition, hop(slot_of[kind], g, a, p, source, target, slot)

    def send(kind, g, a, p):
        condition, copy = route(kind, g, a, p)

        @pl.when(condition)
        def _():
            copy.start()

    def arrive(who, slot, g, a, p):
        held = (has_far, has_last, odd | has_last)[slot]

        @pl.when(who & held)
        def _():
            hop(0, g, a, p, own, partner, slot).wait_recv()

    def wait_for(who, slot, g, a, pieces):
        for p in pieces:
            arrive(who, slot, g, a, p)

    def relay(kind, g, a, pieces):
        who = even if kind < 4 else odd
        source = routes[kind][2]
        for p in pieces:
            if source != own:
                arrive(who, source, g, a, p)
            send(kind, g, a, p)

    def follow(phase, i, g):
        for parity, plan in ((even, EVEN_PLAN), (odd, ODD_PLAN)):
            for (name, step), events in plan.items():
                todo = [
                    (kind, g + (when == "next"), a, pieces)
                    for when, kind, a, pieces in events
                    if g + (when == "next") < groups
                ]
                if name == phase and todo:
                    @pl.when(parity & (i == min(step, n_head - 1)))
                    def _():
                        for event in todo:
                            relay(*event)

    starts = []
    for parity, events in ((even, EVEN_START), (odd, ODD_START)):
        count = 0
        while routes[events[count][0]][2] == own:
            count += 1
        starts.append((parity, events[:count], events[count:]))
    for g in range(groups):
        for a in (K, V):
            loads[g, a].wait()
            if g == 0:
                for _, events, _ in starts:
                    for kind, array, pieces in events:
                        if array == a:
                            relay(kind, g, a, pieces)
            relay(1, g, a, HIGH[a])

    lane = lax.broadcasted_iota(jnp.int32, (1, HD), 1)
    low = jnp.full((1, HD), 1 << 30, jnp.int32)
    high = jnp.full((1, HD), 0, jnp.int32)
    end = jnp.int32(0)
    for d in range(doc_ref.shape[0]):
        start = end
        end = end + doc_ref[d]
        low = jnp.where(lane == d, start, low)
        high = jnp.where(lane == d, end, high)
    first = b * tokens

    def key_docs(i, _):
        rows = i * tile
        pos = first - reach + rows + lax.broadcasted_iota(jnp.int32, (tile, HD), 0)
        same = (pos >= low) & (pos < high)
        kdoc[pl.ds(rows, tile), :] = jnp.where(same, 0.0, FAR).astype(jnp.bfloat16)
        return 0

    lax.fori_loop(0, window // tile, key_docs, 0)

    def query_docs(i, _):
        rows = i * tile
        pos = first + rows + lax.broadcasted_iota(jnp.int32, (tile, HD), 0)
        same = (pos >= low) & (pos < high)
        qdoc[pl.ds(rows, tile), :] = jnp.where(same, 1.0, 0.0).astype(jnp.bfloat16)
        return 0

    lax.fori_loop(0, n_head, query_docs, 0)

    for slot in range(SPAN - 1):
        @pl.when(b < SPAN - 1 - slot)
        def _():
            for g in range(groups):
                for buf in bufs:
                    buf[g, slot * tokens:(slot + 1) * tokens, :] = jnp.zeros((tokens, HD), jnp.bfloat16)

    q_load.wait()

    near = tokens * (SPAN - 2) + tile
    far = tokens
    pairs = n_head // 2

    def tile_at(i):
        return (h // 2 + pairs - 1 - i // 2) % pairs * 2 + (h % 2 + 1 - i % 2) % 2

    def source_at(i):
        return (h // 2 + 1 + i // 2) % pairs * 2 + (h % 2 + 1 - i % 2) % 2

    def columns(g, head):
        return pl.ds(pl.multiple_of((head * groups + g) * width, width), width)

    def deliver(g, i, t):
        return pltpu.make_async_remote_copy(
            src_ref=obuf.at[g, t],
            dst_ref=out_ref.at[:, columns(g, h)],
            send_sem=out_send.at[g, i],
            recv_sem=out_recv.at[g, i],
            device_id={"seq": b, "head": t},
            device_id_type=MESH,
        )

    def receive(g, i):
        source = source_at(i)
        return pltpu.make_async_remote_copy(
            src_ref=obuf.at[g, 0],
            dst_ref=out_ref.at[:, columns(g, source)],
            send_sem=out_send.at[g, i],
            recv_sem=out_recv.at[g, i],
            device_id={"seq": b, "head": source},
            device_id_type=MESH,
        )

    def keep(g):
        return pltpu.make_async_copy(
            obuf.at[g, h], out_ref.at[:, columns(g, h)], own_sem.at[g]
        )

    below = lax.broadcasted_iota(jnp.int32, (tile, tile), 1) <= lax.broadcasted_iota(
        jnp.int32, (tile, tile), 0
    )
    rows_all = GROUP * tile

    def scores_of(g, t, start, size):
        rows = pl.ds(pl.multiple_of(t * tile, tile), tile)
        keys = pl.ds(pl.multiple_of(start, tile), size)
        marks = qdoc[rows, :]
        query_ext = jnp.concatenate([
            jnp.concatenate([qbuf[rows, column:column + HD], marks], 1)
            for column in ((g * GROUP + m) * HD for m in range(GROUP))
        ], 0)
        key_ext = jnp.concatenate([kbuf[g, keys, :], kdoc[keys, :]], 1)
        return lax.dot_general(
            query_ext, key_ext, (((1,), (1,)), ((), ())), preferred_element_type=jnp.float32
        )

    def weigh_near(g, t):
        scores = scores_of(g, t, t * tile + far, near)
        edge = jnp.where(jnp.concatenate([below] * GROUP, 0), scores[:, near - tile:], FAR)
        scores = jnp.concatenate([scores[:, :near - tile], edge], 1)
        largest = jnp.max(scores, axis=1, keepdims=True)
        near_w[g, t] = jnp.exp2((scores - largest) * EXP2_SCALE).astype(jnp.bfloat16)
        peak[g, t] = jnp.broadcast_to(largest, (rows_all, HD))

    def weigh_far(g, t):
        scores = scores_of(g, t, t * tile, far)
        before = peak[g, t]
        largest = jnp.maximum(jnp.max(scores, axis=1, keepdims=True), before)
        fade[g, t] = jnp.exp2((before - largest) * EXP2_SCALE)
        far_w[g, t] = jnp.exp2(
            (scores - jnp.concatenate([largest] * (far // HD), 1)) * EXP2_SCALE
        ).astype(jnp.bfloat16)

    def values_of(g, start, size):
        keys = pl.ds(pl.multiple_of(start, tile), size)
        return jnp.concatenate([vbuf[g, keys, :], jnp.ones((size, HD), jnp.bfloat16)], 1)

    def blend(g, t):
        near_v = values_of(g, t * tile + far, near)
        far_v = values_of(g, t * tile, far)
        for part in range(GROUP // PAIR):
            rows = slice(part * PAIR * tile, (part + 1) * PAIR * tile)
            faded = fade[g, t, rows, :]
            mixed = jnp.dot(near_w[g, t, rows, :], near_v, preferred_element_type=jnp.float32)
            mixed = mixed * jnp.concatenate([faded, faded], 1) + jnp.dot(
                far_w[g, t, rows, :], far_v, preferred_element_type=jnp.float32
            )
            result = (mixed[:, :HD] / mixed[:, HD:]).astype(jnp.bfloat16)
            for m in range(PAIR):
                column = (part * PAIR + m) * HD
                obuf[g, t, :, column:column + HD] = result[m * tile:(m + 1) * tile]

    for parity, _, events in starts:
        @pl.when(parity)
        def _():
            for kind, a, pieces in events:
                relay(kind, 0, a, pieces)

    for g in range(groups):
        wait_for(even, 1, g, K, LOW[K])
        wait_for(odd, 2, g, K, HIGH[K])

        def near_step(i, _):
            weigh_near(g, tile_at(i))
            follow("near", i, g)
            return 0

        lax.fori_loop(0, n_head, near_step, 0)
        wait_for(even, 0, g, K, ALL)
        wait_for(odd, 0, g, K, HIGH[K])

        def far_step(j, _):
            for m in range(2):
                weigh_far(g, tile_at(2 * j + m))
            follow("far", 2 * j + 1, g)
            return 0

        lax.fori_loop(0, n_head // 2, far_step, 0)
        wait_for(even, 1, g, V, LOW[V])
        wait_for(odd, 2, g, V, HIGH[V])
        wait_for(even, 0, g, V, ALL)
        wait_for(odd, 0, g, V, HIGH[V])

        def blend_far(i, _):
            t = tile_at(i)
            blend(g, t)
            deliver(g, i, t).start()
            follow("blend", i, g)
            return 0

        lax.fori_loop(0, n_head // 2, blend_far, 0)

    for g in range(groups):
        def blend_near(i, _):
            t = tile_at(i)
            blend(g, t)

            @pl.when(i < n_head - 1)
            def _():
                deliver(g, i, t).start()

            @pl.when(i == n_head - 1)
            def _():
                keep(g).start()
            return 0

        lax.fori_loop(n_head // 2, n_head, blend_near, 0)

    for kind, (condition, pieces, *_) in routes.items():
        @pl.when(condition)
        def _():
            for g in range(groups):
                for a in (K, V):
                    for p in pieces[a]:
                        route(kind, g, a, p)[1].wait_send()
    for g in range(groups):
        keep(g).wait()
        for i in range(n_head - 1):
            deliver(g, i, tile_at(i)).wait_send()
            receive(g, i).wait_recv()


def per_device(n_seq, n_head, queries, key_rows, value_rows, doc_lengths):
    tokens = queries.shape[0]
    groups = key_rows.shape[1] // HD
    tile = tokens // n_head
    window = SPAN * tokens
    flops = 4 * tokens * (GROUP * groups) * window * HD
    return pl.pallas_call(
        functools.partial(kernel, n_seq, n_head),
        out_shape=pltpu.VMEM((tile, H * HD), jnp.bfloat16),
        in_specs=[pl.BlockSpec(memory_space=pltpu.SMEM)]
        + [pl.BlockSpec(memory_space=pl.ANY)] * 3,
        out_specs=pl.BlockSpec(memory_space=pl.ANY),
        scratch_shapes=[
            pltpu.VMEM((tokens, GROUP * groups * HD), jnp.bfloat16),
            pltpu.VMEM((groups, window, HD), jnp.bfloat16),
            pltpu.VMEM((groups, window, HD), jnp.bfloat16),
            pltpu.VMEM((tokens, HD), jnp.bfloat16),
            pltpu.VMEM((window, HD), jnp.bfloat16),
            pltpu.VMEM((groups, n_head, GROUP * tile, tokens * (SPAN - 2) + tile), jnp.bfloat16),
            pltpu.VMEM((groups, n_head, GROUP * tile, tokens), jnp.bfloat16),
            pltpu.VMEM((groups, n_head, GROUP * tile, HD), jnp.float32),
            pltpu.VMEM((groups, n_head, GROUP * tile, HD), jnp.float32),
            pltpu.VMEM((groups, n_head, tile, GROUP * HD), jnp.bfloat16),
            pltpu.SemaphoreType.DMA((groups + 1, 2)),
            pltpu.SemaphoreType.DMA((5, groups, 2, PIECES)),
            pltpu.SemaphoreType.DMA((SPAN - 1, groups, 2, PIECES)),
            pltpu.SemaphoreType.DMA((groups, n_head - 1)),
            pltpu.SemaphoreType.DMA((groups, n_head - 1)),
            pltpu.SemaphoreType.DMA((groups,)),
        ],
        compiler_params=pltpu.CompilerParams(
            collective_id=0, has_side_effects=True, vmem_limit_bytes=56 << 20
        ),
        cost_estimate=pl.CostEstimate(flops=flops, bytes_accessed=4 << 20, transcendentals=0),
    )(doc_lengths, queries, key_rows, value_rows)


def solution(mesh):
    body = functools.partial(per_device, mesh.shape["seq"], mesh.shape["head"])
    in_specs = (P("seq", "head"), P("seq", "head"), P("seq", "head"), P())
    out_specs = P(("seq", "head"), None)
    return jax.shard_map(body, mesh=mesh, in_specs=in_specs, out_specs=out_specs, check_vma=False)
```

```python
import functools
import math

import jax
import jax.numpy as jnp
from jax import lax
from jax.experimental import pallas as pl
from jax.experimental.pallas import tpu as pltpu
from jax.sharding import PartitionSpec as P

H = 32
KVH = 8
HD = 128
SPAN = 4
FAR = -1e30
PAIR = 2
PIECES = 4
KEYS, VALUES = 0, 1
ALL = (0, 1, 2, 3)
HIGH = ((0, 1, 2, 3), (3,))
LOW = ((), (0, 1, 2))
EVEN_PLAN = {
    ("near", 0): (("next", 0, KEYS, (0, 1, 2, 3)), ("now", 3, VALUES, (1,)),),
    ("near", 1): (("next", 0, VALUES, (0,)), ("now", 3, VALUES, (0,)),),
    ("near", 2): (("next", 0, VALUES, (1,)), ("now", 3, VALUES, (2, 3)),),
    ("far", 1): (("next", 0, VALUES, (2,)), ("next", 2, KEYS, (3, 0, 2, 1)),),
    ("far", 3): (("next", 0, VALUES, (3,)), ("next", 3, KEYS, (1,)),),
    ("blend", 0): (("next", 3, KEYS, (0,)),),
    ("blend", 1): (("next", 2, VALUES, (3,)), ("next", 3, KEYS, (2, 3)),),
}
ODD_PLAN = {
    ("near", 0): (("next", 4, KEYS, (1, 0)), ("now", 5, VALUES, (0, 2)), ("now", 6, VALUES, (0, 1)),),
    ("near", 1): (("now", 5, VALUES, (3,)), ("now", 6, VALUES, (2,)),),
    ("near", 2): (("next", 5, KEYS, (0,)), ("next", 4, KEYS, (2,)), ("next", 5, KEYS, (1,)), ("next", 4, KEYS, (3,)), ("now", 7, VALUES, (0,)),),
    ("near", 3): (("next", 4, VALUES, (1, 0, 2)), ("now", 7, VALUES, (1, 2)),),
    ("far", 1): (("next", 5, KEYS, (2,)),),
    ("far", 3): (("next", 5, KEYS, (3,)),),
    ("blend", 0): (("next", 4, VALUES, (3,)),),
    ("blend", 1): (("next", 5, VALUES, (1,)),),
}
EVEN_START = (
    (0, KEYS, (0, 2, 1, 3)),
    (0, VALUES, (0, 1, 2, 3)),
    (2, KEYS, (0, 2, 3, 1)),
    (2, VALUES, (3,)),
    (3, KEYS, (0, 2, 3, 1)),
)
ODD_START = (
    (4, KEYS, (0, 2, 3, 1)),
    (4, VALUES, (1,)),
    (5, KEYS, (0,)),
    (4, VALUES, (2, 0)),
    (5, KEYS, (2,)),
    (4, VALUES, (3,)),
    (5, KEYS, (3, 1)),
    (5, VALUES, (1,)),
)
GROUP = H // KVH
EXP2_SCALE = 0.08838834764831845 * math.log2(math.e)
MESH = pl.DeviceIdType.MESH


def kernel(
    n_seq, n_head, doc_hbm, q_hbm, k_hbm, v_hbm, out_ref,
    qbuf, kbuf, vbuf, qdoc, kdoc, near_w, far_w, peak, fade, obuf,
    load_sem, send_sem, recv_sem, out_send, out_recv, own_sem, doc_ref, doc_sem,
):
    b = lax.axis_index("seq")
    h = lax.axis_index("head")
    tokens = q_hbm.shape[0]
    groups = k_hbm.shape[1] // HD
    tile = tokens // n_head
    width = GROUP * HD
    window = SPAN * tokens
    reach = (SPAN - 1) * tokens
    own = SPAN - 1
    even = b % 2 == 0
    odd = b % 2 == 1
    bufs = (kbuf, vbuf)
    K, V = KEYS, VALUES

    barrier = pltpu.get_barrier_semaphore()
    partner = b + 1 - 2 * (b % 2)
    has_next = b + 2 < n_seq
    has_last = b >= 2
    has_far = b >= SPAN - 1

    def greet(seq, head):
        pl.semaphore_signal(
            barrier, inc=1, device_id={"seq": seq, "head": head}, device_id_type=MESH
        )

    for condition, seq in ((has_next, b + 2), (has_last, b - 2)):
        @pl.when(condition)
        def _():
            greet(seq, h)
    greet(partner, h)
    for off in range(1, n_head):
        greet(b, (h + off) % n_head)

    doc_load = pltpu.make_async_copy(doc_hbm, doc_ref, doc_sem)
    loads = {}
    for g in range(groups):
        for a, source in enumerate((k_hbm, v_hbm)):
            loads[g, a] = pltpu.make_async_copy(
                source.at[:, pl.ds(g * HD, HD)],
                bufs[a].at[g, pl.ds(reach, tokens), :],
                load_sem.at[g, a],
            )
    for load in loads.values():
        load.start()
    q_load = pltpu.make_async_copy(q_hbm, qbuf, load_sem.at[groups, 0])
    q_load.start()
    doc_load.start()

    pl.semaphore_wait(
        barrier, n_head + jnp.where(has_next, 1, 0) + jnp.where(has_last, 1, 0)
    )

    size = tokens // PIECES

    def hop(kind, g, a, p, source, target, slot):
        return pltpu.make_async_remote_copy(
            src_ref=bufs[a].at[g, pl.ds(source * tokens + p * size, size), :],
            dst_ref=bufs[a].at[g, pl.ds(slot * tokens + p * size, size), :],
            send_sem=send_sem.at[kind, g, a, p],
            recv_sem=recv_sem.at[slot, g, a, p],
            device_id={"seq": target, "head": h},
            device_id_type=MESH,
        )

    routes = {
        0: (even, (ALL, ALL), own, b + 1, 2),
        1: (even & has_next, HIGH, own, b + 2, 1),
        2: (even & has_last, HIGH, 1, b + 1, 0),
        3: (even & has_last & has_next, (ALL, ALL), 2, b + 2, 0),
        4: (odd & has_next, (ALL, ALL), own, b + 2, 1),
        5: (odd & has_last, (ALL, ALL), 1, b - 1, 2),
        6: (odd & has_next, LOW, 2, b + 2, 0),
        7: (odd & has_far, LOW, 0, b - 1, 1),
    }
    slot_of = {0: 0, 1: 1, 2: 2, 3: 3, 4: 1, 5: 2, 6: 3, 7: 4}

    def route(kind, g, a, p):
        condition, _, source, target, slot = routes[kind]
        return condition, hop(slot_of[kind], g, a, p, source, target, slot)

    def send(kind, g, a, p):
        condition, copy = route(kind, g, a, p)

        @pl.when(condition)
        def _():
            copy.start()

    def arrive(who, slot, g, a, p):
        held = (has_far, has_last, odd | has_last)[slot]

        @pl.when(who & held)
        def _():
            hop(0, g, a, p, own, partner, slot).wait_recv()

    def wait_for(who, slot, g, a, pieces):
        for p in pieces:
            arrive(who, slot, g, a, p)

    def relay(kind, g, a, pieces):
        who = even if kind < 4 else odd
        source = routes[kind][2]
        for p in pieces:
            if source != own:
                arrive(who, source, g, a, p)
            send(kind, g, a, p)

    def follow(phase, i, g):
        for parity, plan in ((even, EVEN_PLAN), (odd, ODD_PLAN)):
            for (name, step), events in plan.items():
                todo = [
                    (kind, g + (when == "next"), a, pieces)
                    for when, kind, a, pieces in events
                    if g + (when == "next") < groups
                ]
                if name == phase and todo:
                    @pl.when(parity & (i == min(step, n_head - 1)))
                    def _():
                        for event in todo:
                            relay(*event)

    starts = []
    for parity, events in ((even, EVEN_START), (odd, ODD_START)):
        count = 0
        while routes[events[count][0]][2] == own:
            count += 1
        starts.append((parity, events[:count], events[count:]))
    for g in range(groups):
        for a in (K, V):
            loads[g, a].wait()
            if g == 0:
                for _, events, _ in starts:
                    for kind, array, pieces in events:
                        if array == a:
                            relay(kind, g, a, pieces)
            relay(1, g, a, HIGH[a])

    doc_load.wait()
    lane = lax.broadcasted_iota(jnp.int32, (1, HD), 1)
    low = jnp.full((1, HD), 1 << 30, jnp.int32)
    high = jnp.full((1, HD), 0, jnp.int32)
    end = jnp.int32(0)
    for d in range(doc_ref.shape[0]):
        start = end
        end = end + doc_ref[d]
        low = jnp.where(lane == d, start, low)
        high = jnp.where(lane == d, end, high)
    first = b * tokens

    def key_docs(i, _):
        rows = i * tile
        pos = first - reach + rows + lax.broadcasted_iota(jnp.int32, (tile, HD), 0)
        same = (pos >= low) & (pos < high)
        kdoc[pl.ds(rows, tile), :] = jnp.where(same, 0.0, FAR).astype(jnp.bfloat16)
        return 0

    lax.fori_loop(0, window // tile, key_docs, 0)

    def query_docs(i, _):
        rows = i * tile
        pos = first + rows + lax.broadcasted_iota(jnp.int32, (tile, HD), 0)
        same = (pos >= low) & (pos < high)
        qdoc[pl.ds(rows, tile), :] = jnp.where(same, 1.0, 0.0).astype(jnp.bfloat16)
        return 0

    lax.fori_loop(0, n_head, query_docs, 0)

    for slot in range(SPAN - 1):
        @pl.when(b < SPAN - 1 - slot)
        def _():
            for g in range(groups):
                for buf in bufs:
                    buf[g, slot * tokens:(slot + 1) * tokens, :] = jnp.zeros((tokens, HD), jnp.bfloat16)

    q_load.wait()

    near = tokens * (SPAN - 2) + tile
    far = tokens
    pairs = n_head // 2

    def tile_at(i):
        return (h // 2 + pairs - 1 - i // 2) % pairs * 2 + (h % 2 + 1 - i % 2) % 2

    def source_at(i):
        return (h // 2 + 1 + i // 2) % pairs * 2 + (h % 2 + 1 - i % 2) % 2

    def columns(g, head):
        return pl.ds(pl.multiple_of((head * groups + g) * width, width), width)

    def deliver(g, i, t):
        return pltpu.make_async_remote_copy(
            src_ref=obuf.at[g, t],
            dst_ref=out_ref.at[:, columns(g, h)],
            send_sem=out_send.at[g, i],
            recv_sem=out_recv.at[g, i],
            device_id={"seq": b, "head": t},
            device_id_type=MESH,
        )

    def receive(g, i):
        source = source_at(i)
        return pltpu.make_async_remote_copy(
            src_ref=obuf.at[g, 0],
            dst_ref=out_ref.at[:, columns(g, source)],
            send_sem=out_send.at[g, i],
            recv_sem=out_recv.at[g, i],
            device_id={"seq": b, "head": source},
            device_id_type=MESH,
        )

    def keep(g):
        return pltpu.make_async_copy(
            obuf.at[g, h], out_ref.at[:, columns(g, h)], own_sem.at[g]
        )

    below = lax.broadcasted_iota(jnp.int32, (tile, tile), 1) <= lax.broadcasted_iota(
        jnp.int32, (tile, tile), 0
    )
    rows_all = GROUP * tile

    def scores_of(g, t, start, size):
        rows = pl.ds(pl.multiple_of(t * tile, tile), tile)
        keys = pl.ds(pl.multiple_of(start, tile), size)
        marks = qdoc[rows, :]
        query_ext = jnp.concatenate([
            jnp.concatenate([qbuf[rows, column:column + HD], marks], 1)
            for column in ((g * GROUP + m) * HD for m in range(GROUP))
        ], 0)
        key_ext = jnp.concatenate([kbuf[g, keys, :], kdoc[keys, :]], 1)
        return lax.dot_general(
            query_ext, key_ext, (((1,), (1,)), ((), ())), preferred_element_type=jnp.float32
        )

    def weigh_near(g, t):
        scores = scores_of(g, t, t * tile + far, near)
        edge = jnp.where(jnp.concatenate([below] * GROUP, 0), scores[:, near - tile:], FAR)
        scores = jnp.concatenate([scores[:, :near - tile], edge], 1)
        largest = jnp.max(scores, axis=1, keepdims=True)
        near_w[g, t] = jnp.exp2((scores - largest) * EXP2_SCALE).astype(jnp.bfloat16)
        peak[g, t] = jnp.broadcast_to(largest, (rows_all, HD))

    def weigh_far(g, t):
        scores = scores_of(g, t, t * tile, far)
        before = peak[g, t]
        largest = jnp.maximum(jnp.max(scores, axis=1, keepdims=True), before)
        fade[g, t] = jnp.exp2((before - largest) * EXP2_SCALE)
        far_w[g, t] = jnp.exp2(
            (scores - jnp.concatenate([largest] * (far // HD), 1)) * EXP2_SCALE
        ).astype(jnp.bfloat16)

    def values_of(g, start, size):
        keys = pl.ds(pl.multiple_of(start, tile), size)
        return jnp.concatenate([vbuf[g, keys, :], jnp.ones((size, HD), jnp.bfloat16)], 1)

    def blend(g, t):
        near_v = values_of(g, t * tile + far, near)
        far_v = values_of(g, t * tile, far)
        for part in range(GROUP // PAIR):
            rows = slice(part * PAIR * tile, (part + 1) * PAIR * tile)
            faded = fade[g, t, rows, :]
            mixed = jnp.dot(near_w[g, t, rows, :], near_v, preferred_element_type=jnp.float32)
            mixed = mixed * jnp.concatenate([faded, faded], 1) + jnp.dot(
                far_w[g, t, rows, :], far_v, preferred_element_type=jnp.float32
            )
            result = (mixed[:, :HD] / mixed[:, HD:]).astype(jnp.bfloat16)
            for m in range(PAIR):
                column = (part * PAIR + m) * HD
                obuf[g, t, :, column:column + HD] = result[m * tile:(m + 1) * tile]

    for parity, _, events in starts:
        @pl.when(parity)
        def _():
            for kind, a, pieces in events:
                relay(kind, 0, a, pieces)

    for g in range(groups):
        wait_for(even, 1, g, K, LOW[K])
        wait_for(odd, 2, g, K, HIGH[K])

        def near_step(i, _):
            weigh_near(g, tile_at(i))
            follow("near", i, g)
            return 0

        lax.fori_loop(0, n_head, near_step, 0)
        wait_for(even, 0, g, K, ALL)
        wait_for(odd, 0, g, K, HIGH[K])

        def far_step(j, _):
            for m in range(2):
                weigh_far(g, tile_at(2 * j + m))
            follow("far", 2 * j + 1, g)
            return 0

        lax.fori_loop(0, n_head // 2, far_step, 0)
        wait_for(even, 1, g, V, LOW[V])
        wait_for(odd, 2, g, V, HIGH[V])
        wait_for(even, 0, g, V, ALL)
        wait_for(odd, 0, g, V, HIGH[V])

        def blend_far(i, _):
            t = tile_at(i)
            blend(g, t)
            deliver(g, i, t).start()
            follow("blend", i, g)
            return 0

        lax.fori_loop(0, n_head // 2, blend_far, 0)

    for g in range(groups):
        def blend_near(i, _):
            t = tile_at(i)
            blend(g, t)

            @pl.when(i < n_head - 1)
            def _():
                deliver(g, i, t).start()

            @pl.when(i == n_head - 1)
            def _():
                keep(g).start()
            return 0

        lax.fori_loop(n_head // 2, n_head, blend_near, 0)

    for kind, (condition, pieces, *_) in routes.items():
        @pl.when(condition)
        def _():
            for g in range(groups):
                for a in (K, V):
                    for p in pieces[a]:
                        route(kind, g, a, p)[1].wait_send()
    for g in range(groups):
        keep(g).wait()
        for i in range(n_head - 1):
            deliver(g, i, tile_at(i)).wait_send()
            receive(g, i).wait_recv()


def per_device(n_seq, n_head, queries, key_rows, value_rows, doc_lengths):
    tokens = queries.shape[0]
    groups = key_rows.shape[1] // HD
    tile = tokens // n_head
    window = SPAN * tokens
    flops = 4 * tokens * (GROUP * groups) * window * HD
    return pl.pallas_call(
        functools.partial(kernel, n_seq, n_head),
        out_shape=pltpu.VMEM((tile, H * HD), jnp.bfloat16),
        in_specs=[pl.BlockSpec(memory_space=pl.ANY)] * 4,
        out_specs=pl.BlockSpec(memory_space=pl.ANY),
        scratch_shapes=[
            pltpu.VMEM((tokens, GROUP * groups * HD), jnp.bfloat16),
            pltpu.VMEM((groups, window, HD), jnp.bfloat16),
            pltpu.VMEM((groups, window, HD), jnp.bfloat16),
            pltpu.VMEM((tokens, HD), jnp.bfloat16),
            pltpu.VMEM((window, HD), jnp.bfloat16),
            pltpu.VMEM((groups, n_head, GROUP * tile, tokens * (SPAN - 2) + tile), jnp.bfloat16),
            pltpu.VMEM((groups, n_head, GROUP * tile, tokens), jnp.bfloat16),
            pltpu.VMEM((groups, n_head, GROUP * tile, HD), jnp.float32),
            pltpu.VMEM((groups, n_head, GROUP * tile, HD), jnp.float32),
            pltpu.VMEM((groups, n_head, tile, GROUP * HD), jnp.bfloat16),
            pltpu.SemaphoreType.DMA((groups + 1, 2)),
            pltpu.SemaphoreType.DMA((5, groups, 2, PIECES)),
            pltpu.SemaphoreType.DMA((SPAN - 1, groups, 2, PIECES)),
            pltpu.SemaphoreType.DMA((groups, n_head - 1)),
            pltpu.SemaphoreType.DMA((groups, n_head - 1)),
            pltpu.SemaphoreType.DMA((groups,)),
            pltpu.SMEM(doc_lengths.shape, jnp.int32),
            pltpu.SemaphoreType.DMA,
        ],
        compiler_params=pltpu.CompilerParams(
            collective_id=0, has_side_effects=True, vmem_limit_bytes=56 << 20
        ),
        cost_estimate=pl.CostEstimate(flops=flops, bytes_accessed=4 << 20, transcendentals=0),
    )(doc_lengths, queries, key_rows, value_rows)


def solution(mesh):
    body = functools.partial(per_device, mesh.shape["seq"], mesh.shape["head"])
    in_specs = (P("seq", "head"), P("seq", "head"), P("seq", "head"), P())
    out_specs = P(("seq", "head"), None)
    return jax.shard_map(body, mesh=mesh, in_specs=in_specs, out_specs=out_specs, check_vma=False)
```

```python
import functools
import math

import jax
import jax.numpy as jnp
from jax import lax
from jax.experimental import pallas as pl
from jax.experimental.pallas import tpu as pltpu
from jax.sharding import PartitionSpec as P

H = 32
KVH = 8
HD = 128
SPAN = 4
FAR = -1e30
PAIR = 2
PIECES = 4
KEYS, VALUES = 0, 1
ALL = (0, 1, 2, 3)
HIGH = ((0, 1, 2, 3), (2, 3))
LOW = ((), (0, 1))
DIAG = ((), (3,))
REST = tuple(tuple(p for p in ALL if p not in some) for some in DIAG)
EVEN_PLAN = {
    ("near", 0): (("next", 0, KEYS, (0, 1, 3)), ("now", 3, VALUES, (0,)),),
    ("near", 1): (("next", 0, KEYS, (2,)), ("now", 3, VALUES, (2,)),),
    ("near", 2): (("next", 0, VALUES, (0, 1)), ("next", 2, KEYS, (2, 0)), ("now", 3, VALUES, (1,)),),
    ("near", 3): (("next", 2, KEYS, (1, 3)),),
    ("far", 1): (("next", 0, VALUES, (3,)),),
    ("far", 3): (("next", 3, KEYS, (2,)), ("next", 0, VALUES, (2,)),),
    ("blend", 0): (("next", 3, KEYS, (0,)),),
    ("blend", 1): (("next", 2, VALUES, (2, 3)), ("next", 3, KEYS, (3, 1)),),
}
ODD_PLAN = {
    ("near", 0): (("next", 4, KEYS, (0,)), ("now", 6, VALUES, (0,)), ("now", 5, VALUES, (1,)), ("now", 6, VALUES, (1,)),),
    ("near", 1): (("now", 5, VALUES, (3,)),),
    ("near", 2): (("next", 5, KEYS, (0,)), ("next", 4, KEYS, (2, 1)), ("now", 7, VALUES, (0, 1)),),
    ("near", 3): (("next", 4, KEYS, (3,)),),
    ("far", 1): (("next", 5, KEYS, (2,)), ("next", 4, VALUES, (0, 2)), ("next", 5, KEYS, (1,)),),
    ("far", 3): (("next", 5, KEYS, (3,)), ("next", 4, VALUES, (1,)),),
    ("blend", 0): (("next", 5, VALUES, (0,)),),
    ("blend", 1): (("next", 4, VALUES, (3,)), ("next", 5, VALUES, (2,)),),
}
EVEN_START = (
    (0, KEYS, (3, 2, 0, 1)),
    (0, VALUES, (1, 0, 3)),
    (2, KEYS, (0, 1)),
    (0, VALUES, (2,)),
    (2, KEYS, (3, 2)),
    (2, VALUES, (2,)),
    (3, KEYS, (1,)),
    (2, VALUES, (3,)),
    (3, KEYS, (0, 3, 2)),
)
ODD_START = (
    (4, KEYS, (0, 1, 3)),
    (4, VALUES, (0,)),
    (4, KEYS, (2,)),
    (4, VALUES, (2,)),
    (5, KEYS, (1,)),
    (4, VALUES, (1, 3)),
    (5, KEYS, (3, 0, 2)),
    (5, VALUES, (0, 2)),
)
GROUP = H // KVH
EXP2_SCALE = 0.08838834764831845 * math.log2(math.e)
MESH = pl.DeviceIdType.MESH


def kernel(
    n_seq, n_head, doc_hbm, q_hbm, k_hbm, v_hbm, out_ref,
    qbuf, kbuf, vbuf, qdoc, kdoc, near_w, far_w, peak, fade, obuf,
    load_sem, send_sem, recv_sem, out_send, out_recv, own_sem, doc_ref, doc_sem,
):
    b = lax.axis_index("seq")
    h = lax.axis_index("head")
    tokens = q_hbm.shape[0]
    groups = k_hbm.shape[1] // HD
    tile = tokens // n_head
    width = GROUP * HD
    window = SPAN * tokens
    reach = (SPAN - 1) * tokens
    own = SPAN - 1
    even = b % 2 == 0
    odd = b % 2 == 1
    bufs = (kbuf, vbuf)
    K, V = KEYS, VALUES

    barrier = pltpu.get_barrier_semaphore()
    partner = b + 1 - 2 * (b % 2)
    has_next = b + 2 < n_seq
    has_last = b >= 2
    has_far = b >= SPAN - 1
    outer = b - 1 + 2 * (b % 2)
    has_outer = (outer >= 0) & (outer < n_seq)

    def greet(seq, head):
        pl.semaphore_signal(
            barrier, inc=1, device_id={"seq": seq, "head": head}, device_id_type=MESH
        )

    for condition, seq in ((has_next, b + 2), (has_last, b - 2), (has_outer, outer)):
        @pl.when(condition)
        def _():
            greet(seq, h)
    greet(partner, h)
    for off in range(1, n_head):
        greet(b, (h + off) % n_head)

    doc_load = pltpu.make_async_copy(doc_hbm, doc_ref, doc_sem)
    loads = {}
    for g in range(groups):
        for a, source in enumerate((k_hbm, v_hbm)):
            loads[g, a] = pltpu.make_async_copy(
                source.at[:, pl.ds(g * HD, HD)],
                bufs[a].at[g, pl.ds(reach, tokens), :],
                load_sem.at[g, a],
            )
    for load in loads.values():
        load.start()
    q_load = pltpu.make_async_copy(q_hbm, qbuf, load_sem.at[groups, 0])
    q_load.start()
    doc_load.start()

    beyond = sum(jnp.where(c, 1, 0) for c in (has_next, has_last, has_outer))
    pl.semaphore_wait(barrier, n_head + beyond)

    size = tokens // PIECES

    def hop(kind, g, a, p, source, target, slot):
        return pltpu.make_async_remote_copy(
            src_ref=bufs[a].at[g, pl.ds(source * tokens + p * size, size), :],
            dst_ref=bufs[a].at[g, pl.ds(slot * tokens + p * size, size), :],
            send_sem=send_sem.at[kind, g, a, p],
            recv_sem=recv_sem.at[slot, g, a, p],
            device_id={"seq": target, "head": h},
            device_id_type=MESH,
        )

    routes = {
        0: (even, (ALL, ALL), own, b + 1, 2),
        1: (even & has_next, HIGH, own, b + 2, 1),
        2: (even & has_last, HIGH, 1, b + 1, 0),
        3: (even & has_last & has_next, REST, 2, b + 2, 0),
        4: (odd & has_next, (ALL, ALL), own, b + 2, 1),
        5: (odd & has_last, (ALL, ALL), 1, b - 1, 2),
        6: (odd & has_next, LOW, 2, b + 2, 0),
        7: (odd & has_far, LOW, 0, b - 1, 1),
        8: (odd & has_last & has_outer, DIAG, 1, b + 1, 0),
    }
    slot_of = {0: 0, 1: 1, 2: 2, 3: 3, 4: 1, 5: 2, 6: 3, 7: 4, 8: 0}

    def route(kind, g, a, p):
        condition, _, source, target, slot = routes[kind]
        return condition, hop(slot_of[kind], g, a, p, source, target, slot)

    def send(kind, g, a, p):
        condition, copy = route(kind, g, a, p)

        @pl.when(condition)
        def _():
            copy.start()

    def arrive(who, slot, g, a, p):
        held = (has_far, has_last, odd | has_last)[slot]

        @pl.when(who & held)
        def _():
            hop(0, g, a, p, own, partner, slot).wait_recv()

    def wait_for(who, slot, g, a, pieces):
        for p in pieces:
            arrive(who, slot, g, a, p)

    def relay(kind, g, a, pieces):
        who = even if kind < 4 else odd
        source = routes[kind][2]
        for p in pieces:
            if source != own:
                arrive(who, source, g, a, p)
            send(kind, g, a, p)
            if kind == 5 and p in DIAG[a]:
                send(8, g, a, p)

    def follow(phase, i, g):
        for parity, plan in ((even, EVEN_PLAN), (odd, ODD_PLAN)):
            for (name, step), events in plan.items():
                todo = [
                    (kind, g + (when == "next"), a, pieces)
                    for when, kind, a, pieces in events
                    if g + (when == "next") < groups
                ]
                if name == phase and todo:
                    @pl.when(parity & (i == min(step, n_head - 1)))
                    def _():
                        for event in todo:
                            relay(*event)

    starts = []
    for parity, events in ((even, EVEN_START), (odd, ODD_START)):
        count = 0
        while routes[events[count][0]][2] == own:
            count += 1
        starts.append((parity, events[:count], events[count:]))
    for g in range(groups):
        for a in (K, V):
            loads[g, a].wait()
            if g == 0:
                for _, events, _ in starts:
                    for kind, array, pieces in events:
                        if array == a:
                            relay(kind, g, a, pieces)
            relay(1, g, a, HIGH[a])

    doc_load.wait()
    lane = lax.broadcasted_iota(jnp.int32, (1, HD), 1)
    low = jnp.full((1, HD), 1 << 30, jnp.int32)
    high = jnp.full((1, HD), 0, jnp.int32)
    end = jnp.int32(0)
    for d in range(doc_ref.shape[0]):
        start = end
        end = end + doc_ref[d]
        low = jnp.where(lane == d, start, low)
        high = jnp.where(lane == d, end, high)
    first = b * tokens

    def key_docs(i, _):
        rows = i * tile
        pos = first - reach + rows + lax.broadcasted_iota(jnp.int32, (tile, HD), 0)
        same = (pos >= low) & (pos < high)
        kdoc[pl.ds(rows, tile), :] = jnp.where(same, 0.0, FAR).astype(jnp.bfloat16)
        return 0

    lax.fori_loop(0, window // tile, key_docs, 0)

    def query_docs(i, _):
        rows = i * tile
        pos = first + rows + lax.broadcasted_iota(jnp.int32, (tile, HD), 0)
        same = (pos >= low) & (pos < high)
        qdoc[pl.ds(rows, tile), :] = jnp.where(same, 1.0, 0.0).astype(jnp.bfloat16)
        return 0

    lax.fori_loop(0, n_head, query_docs, 0)

    for slot in range(SPAN - 1):
        @pl.when(b < SPAN - 1 - slot)
        def _():
            for g in range(groups):
                for buf in bufs:
                    buf[g, slot * tokens:(slot + 1) * tokens, :] = jnp.zeros((tokens, HD), jnp.bfloat16)

    q_load.wait()

    near = tokens * (SPAN - 2) + tile
    far = tokens
    pairs = n_head // 2

    def tile_at(i):
        return (h // 2 + pairs - 1 - i // 2) % pairs * 2 + (h % 2 + 1 - i % 2) % 2

    def source_at(i):
        return (h // 2 + 1 + i // 2) % pairs * 2 + (h % 2 + 1 - i % 2) % 2

    def columns(g, head):
        return pl.ds(pl.multiple_of((head * groups + g) * width, width), width)

    def deliver(g, i, t):
        return pltpu.make_async_remote_copy(
            src_ref=obuf.at[g, t],
            dst_ref=out_ref.at[:, columns(g, h)],
            send_sem=out_send.at[g, i],
            recv_sem=out_recv.at[g, i],
            device_id={"seq": b, "head": t},
            device_id_type=MESH,
        )

    def receive(g, i):
        source = source_at(i)
        return pltpu.make_async_remote_copy(
            src_ref=obuf.at[g, 0],
            dst_ref=out_ref.at[:, columns(g, source)],
            send_sem=out_send.at[g, i],
            recv_sem=out_recv.at[g, i],
            device_id={"seq": b, "head": source},
            device_id_type=MESH,
        )

    def keep(g):
        return pltpu.make_async_copy(
            obuf.at[g, h], out_ref.at[:, columns(g, h)], own_sem.at[g]
        )

    below = lax.broadcasted_iota(jnp.int32, (tile, tile), 1) <= lax.broadcasted_iota(
        jnp.int32, (tile, tile), 0
    )
    rows_all = GROUP * tile

    def scores_of(g, t, start, size):
        rows = pl.ds(pl.multiple_of(t * tile, tile), tile)
        keys = pl.ds(pl.multiple_of(start, tile), size)
        marks = qdoc[rows, :]
        query_ext = jnp.concatenate([
            jnp.concatenate([qbuf[rows, column:column + HD], marks], 1)
            for column in ((g * GROUP + m) * HD for m in range(GROUP))
        ], 0)
        key_ext = jnp.concatenate([kbuf[g, keys, :], kdoc[keys, :]], 1)
        return lax.dot_general(
            query_ext, key_ext, (((1,), (1,)), ((), ())), preferred_element_type=jnp.float32
        )

    def weigh_near(g, t):
        scores = scores_of(g, t, t * tile + far, near)
        edge = jnp.where(jnp.concatenate([below] * GROUP, 0), scores[:, near - tile:], FAR)
        scores = jnp.concatenate([scores[:, :near - tile], edge], 1)
        largest = jnp.max(scores, axis=1, keepdims=True)
        near_w[g, t] = jnp.exp2((scores - largest) * EXP2_SCALE).astype(jnp.bfloat16)
        peak[g, t] = jnp.broadcast_to(largest, (rows_all, HD))

    def weigh_far(g, t):
        scores = scores_of(g, t, t * tile, far)
        before = peak[g, t]
        largest = jnp.maximum(jnp.max(scores, axis=1, keepdims=True), before)
        fade[g, t] = jnp.exp2((before - largest) * EXP2_SCALE)
        far_w[g, t] = jnp.exp2(
            (scores - jnp.concatenate([largest] * (far // HD), 1)) * EXP2_SCALE
        ).astype(jnp.bfloat16)

    def values_of(g, start, size):
        keys = pl.ds(pl.multiple_of(start, tile), size)
        return jnp.concatenate([vbuf[g, keys, :], jnp.ones((size, HD), jnp.bfloat16)], 1)

    def blend(g, t):
        near_v = values_of(g, t * tile + far, near)
        far_v = values_of(g, t * tile, far)
        for part in range(GROUP // PAIR):
            rows = slice(part * PAIR * tile, (part + 1) * PAIR * tile)
            faded = fade[g, t, rows, :]
            mixed = jnp.dot(near_w[g, t, rows, :], near_v, preferred_element_type=jnp.float32)
            mixed = mixed * jnp.concatenate([faded, faded], 1) + jnp.dot(
                far_w[g, t, rows, :], far_v, preferred_element_type=jnp.float32
            )
            result = (mixed[:, :HD] / mixed[:, HD:]).astype(jnp.bfloat16)
            for m in range(PAIR):
                column = (part * PAIR + m) * HD
                obuf[g, t, :, column:column + HD] = result[m * tile:(m + 1) * tile]

    for parity, _, events in starts:
        @pl.when(parity)
        def _():
            for kind, a, pieces in events:
                relay(kind, 0, a, pieces)

    for g in range(groups):
        later = g + 1 < groups
        wait_for(even, 1, g, K, LOW[K])
        wait_for(odd, 2, g, K, HIGH[K])

        def near_step(i, _):
            if later:
                weigh_near(g, tile_at(i))
            else:
                @pl.when(i < n_head // 2)
                def _():
                    weigh_near(g, tile_at(i))
            follow("near", i, g)
            return 0

        lax.fori_loop(0, n_head, near_step, 0)
        wait_for(even, 0, g, K, ALL)
        wait_for(odd, 0, g, K, HIGH[K])

        def far_step(j, _):
            if later:
                for m in range(2):
                    weigh_far(g, tile_at(2 * j + m))
            else:
                @pl.when(j < n_head // 4)
                def _():
                    for m in range(2):
                        weigh_far(g, tile_at(2 * j + m))
            follow("far", 2 * j + 1, g)
            return 0

        lax.fori_loop(0, n_head // 2, far_step, 0)
        wait_for(even, 1, g, V, LOW[V])
        wait_for(odd, 2, g, V, HIGH[V])
        wait_for(even, 0, g, V, ALL)
        wait_for(even, 2, g, V, DIAG[V])
        wait_for(odd, 0, g, V, HIGH[V])

        def blend_far(i, _):
            t = tile_at(i)
            blend(g, t)
            deliver(g, i, t).start()
            follow("blend", i, g)
            return 0

        lax.fori_loop(0, n_head // 2, blend_far, 0)

    for g in range(groups):
        def blend_near(i, _):
            t = tile_at(i)
            if g + 1 == groups:
                weigh_near(g, t)
                weigh_far(g, t)
            blend(g, t)

            @pl.when(i < n_head - 1)
            def _():
                deliver(g, i, t).start()

            @pl.when(i == n_head - 1)
            def _():
                keep(g).start()
            return 0

        lax.fori_loop(n_head // 2, n_head, blend_near, 0)

    for kind, (condition, pieces, *_) in routes.items():
        @pl.when(condition)
        def _():
            for g in range(groups):
                for a in (K, V):
                    for p in pieces[a]:
                        route(kind, g, a, p)[1].wait_send()
    for g in range(groups):
        keep(g).wait()
        for i in range(n_head - 1):
            deliver(g, i, tile_at(i)).wait_send()
            receive(g, i).wait_recv()


def per_device(n_seq, n_head, queries, key_rows, value_rows, doc_lengths):
    tokens = queries.shape[0]
    groups = key_rows.shape[1] // HD
    tile = tokens // n_head
    window = SPAN * tokens
    flops = 4 * tokens * (GROUP * groups) * window * HD
    return pl.pallas_call(
        functools.partial(kernel, n_seq, n_head),
        out_shape=pltpu.VMEM((tile, H * HD), jnp.bfloat16),
        in_specs=[pl.BlockSpec(memory_space=pl.ANY)] * 4,
        out_specs=pl.BlockSpec(memory_space=pl.ANY),
        scratch_shapes=[
            pltpu.VMEM((tokens, GROUP * groups * HD), jnp.bfloat16),
            pltpu.VMEM((groups, window, HD), jnp.bfloat16),
            pltpu.VMEM((groups, window, HD), jnp.bfloat16),
            pltpu.VMEM((tokens, HD), jnp.bfloat16),
            pltpu.VMEM((window, HD), jnp.bfloat16),
            pltpu.VMEM((groups, n_head, GROUP * tile, tokens * (SPAN - 2) + tile), jnp.bfloat16),
            pltpu.VMEM((groups, n_head, GROUP * tile, tokens), jnp.bfloat16),
            pltpu.VMEM((groups, n_head, GROUP * tile, HD), jnp.float32),
            pltpu.VMEM((groups, n_head, GROUP * tile, HD), jnp.float32),
            pltpu.VMEM((groups, n_head, tile, GROUP * HD), jnp.bfloat16),
            pltpu.SemaphoreType.DMA((groups + 1, 2)),
            pltpu.SemaphoreType.DMA((5, groups, 2, PIECES)),
            pltpu.SemaphoreType.DMA((SPAN - 1, groups, 2, PIECES)),
            pltpu.SemaphoreType.DMA((groups, n_head - 1)),
            pltpu.SemaphoreType.DMA((groups, n_head - 1)),
            pltpu.SemaphoreType.DMA((groups,)),
            pltpu.SMEM(doc_lengths.shape, jnp.int32),
            pltpu.SemaphoreType.DMA,
        ],
        compiler_params=pltpu.CompilerParams(
            collective_id=0, has_side_effects=True, vmem_limit_bytes=56 << 20
        ),
        cost_estimate=pl.CostEstimate(flops=flops, bytes_accessed=4 << 20, transcendentals=0),
    )(doc_lengths, queries, key_rows, value_rows)


def solution(mesh):
    body = functools.partial(per_device, mesh.shape["seq"], mesh.shape["head"])
    in_specs = (P("seq", "head"), P("seq", "head"), P("seq", "head"), P())
    out_specs = P(("seq", "head"), None)
    return jax.shard_map(body, mesh=mesh, in_specs=in_specs, out_specs=out_specs, check_vma=False)
```

```python
import functools
import math

import jax
import jax.numpy as jnp
from jax import lax
from jax.experimental import pallas as pl
from jax.experimental.pallas import tpu as pltpu
from jax.sharding import PartitionSpec as P

H = 32
KVH = 8
HD = 128
SPAN = 4
FAR = -1e30
PAIR = 2
PIECES = 4
KEYS, VALUES = 0, 1
ALL = (0, 1, 2, 3)
HIGH = ((0, 1, 2, 3), (2, 3))
LOW = ((), (0, 1))
DIAG = ((), (3,))
REST = tuple(tuple(p for p in ALL if p not in some) for some in DIAG)
EVEN_PLAN = {
    ("near", 0): (("next", 0, KEYS, (0, 1, 2, 3)), ("next", 0, VALUES, (0, 1)), ("next", 2, KEYS, (0,)), ("now", 3, VALUES, (0,)),),
    ("near", 2): (("next", 2, KEYS, (1,)), ("now", 3, VALUES, (1, 2)),),
    ("near", 3): (("next", 2, VALUES, (3,)),),
    ("far", 1): (("next", 3, KEYS, (2,)), ("next", 2, KEYS, (2,)),),
    ("far", 3): (("next", 2, KEYS, (3,)), ("next", 2, VALUES, (2,)),),
    ("blend", 0): (("next", 0, VALUES, (3, 2)), ("next", 3, KEYS, (3,)),),
    ("blend", 1): (("next", 3, KEYS, (0, 1)),),
}
ODD_PLAN = {
    ("near", 0): (("next", 4, KEYS, (2,)), ("now", 5, VALUES, (1,)), ("now", 6, VALUES, (0, 1)),),
    ("near", 1): (("now", 5, VALUES, (3,)),),
    ("near", 2): (("next", 4, KEYS, (0,)), ("next", 4, VALUES, (2,)),),
    ("near", 3): (("next", 4, KEYS, (3,)), ("now", 7, VALUES, (0, 1)),),
    ("far", 1): (("next", 5, KEYS, (2,)), ("next", 4, KEYS, (1,)),),
    ("far", 3): (("next", 5, KEYS, (0,)), ("next", 4, VALUES, (0,)),),
    ("blend", 0): (("next", 4, VALUES, (1,)), ("next", 5, KEYS, (3,)), ("next", 4, VALUES, (3,)),),
    ("blend", 1): (("next", 5, KEYS, (1,)), ("next", 5, VALUES, (0, 2)),),
}
EVEN_START = (
    (0, KEYS, (2, 3, 1, 0)),
    (0, VALUES, (0, 1)),
    (2, KEYS, (1, 0, 3)),
    (2, VALUES, (2,)),
    (2, KEYS, (2,)),
    (0, VALUES, (2,)),
    (2, VALUES, (3,)),
    (0, VALUES, (3,)),
    (3, KEYS, (1, 0, 2, 3)),
)
ODD_START = (
    (4, KEYS, (0, 1, 3, 2)),
    (4, VALUES, (0,)),
    (5, KEYS, (0, 1)),
    (4, VALUES, (2, 1)),
    (5, KEYS, (3, 2)),
    (4, VALUES, (3,)),
    (5, VALUES, (0, 2)),
)
GROUP = H // KVH
EXP2_SCALE = 0.08838834764831845 * math.log2(math.e)
MESH = pl.DeviceIdType.MESH


def kernel(
    n_seq, n_head, doc_hbm, q_hbm, k_hbm, v_hbm, out_ref,
    qbuf, kbuf, vbuf, qdoc, kdoc, near_w, far_w, peak, fade, obuf,
    load_sem, send_sem, recv_sem, out_send, out_recv, own_sem, doc_ref, doc_sem,
):
    b = lax.axis_index("seq")
    h = lax.axis_index("head")
    tokens = q_hbm.shape[0]
    groups = k_hbm.shape[1] // HD
    tile = tokens // n_head
    width = GROUP * HD
    window = SPAN * tokens
    reach = (SPAN - 1) * tokens
    own = SPAN - 1
    even = b % 2 == 0
    odd = b % 2 == 1
    bufs = (kbuf, vbuf)
    K, V = KEYS, VALUES

    barrier = pltpu.get_barrier_semaphore()
    partner = b + 1 - 2 * (b % 2)
    has_next = b + 2 < n_seq
    has_last = b >= 2
    has_far = b >= SPAN - 1
    outer = b - 1 + 2 * (b % 2)
    has_outer = (outer >= 0) & (outer < n_seq)

    def greet(seq, head):
        pl.semaphore_signal(
            barrier, inc=1, device_id={"seq": seq, "head": head}, device_id_type=MESH
        )

    for condition, seq in ((has_next, b + 2), (has_last, b - 2), (has_outer, outer)):
        @pl.when(condition)
        def _():
            greet(seq, h)
    greet(partner, h)
    for off in range(1, n_head):
        greet(b, (h + off) % n_head)

    doc_load = pltpu.make_async_copy(doc_hbm, doc_ref, doc_sem)
    loads = {}
    for g in range(groups):
        for a, source in enumerate((k_hbm, v_hbm)):
            loads[g, a] = pltpu.make_async_copy(
                source.at[:, pl.ds(g * HD, HD)],
                bufs[a].at[g, pl.ds(reach, tokens), :],
                load_sem.at[g, a],
            )
    for load in loads.values():
        load.start()
    q_load = pltpu.make_async_copy(q_hbm, qbuf, load_sem.at[groups, 0])
    q_load.start()
    doc_load.start()

    beyond = sum(jnp.where(c, 1, 0) for c in (has_next, has_last, has_outer))
    pl.semaphore_wait(barrier, n_head + beyond)

    size = tokens // PIECES

    def hop(kind, g, a, p, source, target, slot):
        return pltpu.make_async_remote_copy(
            src_ref=bufs[a].at[g, pl.ds(source * tokens + p * size, size), :],
            dst_ref=bufs[a].at[g, pl.ds(slot * tokens + p * size, size), :],
            send_sem=send_sem.at[kind, g, a, p],
            recv_sem=recv_sem.at[slot, g, a, p],
            device_id={"seq": target, "head": h},
            device_id_type=MESH,
        )

    routes = {
        0: (even, (ALL, ALL), own, b + 1, 2),
        1: (even & has_next, HIGH, own, b + 2, 1),
        2: (even & has_last, HIGH, 1, b + 1, 0),
        3: (even & has_last & has_next, REST, 2, b + 2, 0),
        4: (odd & has_next, (ALL, ALL), own, b + 2, 1),
        5: (odd & has_last, (ALL, ALL), 1, b - 1, 2),
        6: (odd & has_next, LOW, 2, b + 2, 0),
        7: (odd & has_far, LOW, 0, b - 1, 1),
        8: (odd & has_last & has_outer, DIAG, 1, b + 1, 0),
    }
    slot_of = {0: 0, 1: 1, 2: 2, 3: 3, 4: 1, 5: 2, 6: 3, 7: 4, 8: 0}

    def route(kind, g, a, p):
        condition, _, source, target, slot = routes[kind]
        return condition, hop(slot_of[kind], g, a, p, source, target, slot)

    def send(kind, g, a, p):
        condition, copy = route(kind, g, a, p)

        @pl.when(condition)
        def _():
            copy.start()

    def arrive(who, slot, g, a, p):
        held = (has_far, has_last, odd | has_last)[slot]

        @pl.when(who & held)
        def _():
            hop(0, g, a, p, own, partner, slot).wait_recv()

    def wait_for(who, slot, g, a, pieces):
        for p in pieces:
            arrive(who, slot, g, a, p)

    def relay(kind, g, a, pieces):
        who = even if kind < 4 else odd
        source = routes[kind][2]
        for p in pieces:
            if source != own:
                arrive(who, source, g, a, p)
            send(kind, g, a, p)
            if kind == 5 and p in DIAG[a]:
                send(8, g, a, p)

    def follow(phase, i, g):
        for parity, plan in ((even, EVEN_PLAN), (odd, ODD_PLAN)):
            for (name, step), events in plan.items():
                todo = [
                    (kind, g + (when == "next"), a, pieces)
                    for when, kind, a, pieces in events
                    if g + (when == "next") < groups
                ]
                if name == phase and todo:
                    @pl.when(parity & (i == min(step, n_head - 1)))
                    def _():
                        for event in todo:
                            relay(*event)

    starts = []
    for parity, events in ((even, EVEN_START), (odd, ODD_START)):
        count = 0
        while routes[events[count][0]][2] == own:
            count += 1
        starts.append((parity, events[:count], events[count:]))
    for g in range(groups):
        for a in (K, V):
            loads[g, a].wait()
            if g == 0:
                for _, events, _ in starts:
                    for kind, array, pieces in events:
                        if array == a:
                            relay(kind, g, a, pieces)
            relay(1, g, a, HIGH[a])

    doc_load.wait()
    lane = lax.broadcasted_iota(jnp.int32, (1, HD), 1)
    low = jnp.full((1, HD), 1 << 30, jnp.int32)
    high = jnp.full((1, HD), 0, jnp.int32)
    end = jnp.int32(0)
    for d in range(doc_ref.shape[0]):
        start = end
        end = end + doc_ref[d]
        low = jnp.where(lane == d, start, low)
        high = jnp.where(lane == d, end, high)
    first = b * tokens

    def key_docs(i, _):
        rows = i * tile
        pos = first - reach + rows + lax.broadcasted_iota(jnp.int32, (tile, HD), 0)
        same = (pos >= low) & (pos < high)
        kdoc[pl.ds(rows, tile), :] = jnp.where(same, 0.0, FAR).astype(jnp.bfloat16)
        return 0

    lax.fori_loop(0, window // tile, key_docs, 0)

    def query_docs(i, _):
        rows = i * tile
        pos = first + rows + lax.broadcasted_iota(jnp.int32, (tile, HD), 0)
        same = (pos >= low) & (pos < high)
        qdoc[pl.ds(rows, tile), :] = jnp.where(same, 1.0, 0.0).astype(jnp.bfloat16)
        return 0

    lax.fori_loop(0, n_head, query_docs, 0)

    for slot in range(SPAN - 1):
        @pl.when(b < SPAN - 1 - slot)
        def _():
            for g in range(groups):
                for buf in bufs:
                    buf[g, slot * tokens:(slot + 1) * tokens, :] = jnp.zeros((tokens, HD), jnp.bfloat16)

    q_load.wait()

    near = tokens * (SPAN - 2) + tile
    far = tokens
    pairs = n_head // 2

    def tile_at(i):
        return (h // 2 + pairs - 1 - i // 2) % pairs * 2 + (h % 2 + 1 - i % 2) % 2

    def source_at(i):
        return (h // 2 + 1 + i // 2) % pairs * 2 + (h % 2 + 1 - i % 2) % 2

    def columns(g, head):
        return pl.ds(pl.multiple_of((head * groups + g) * width, width), width)

    def deliver(g, i, t):
        return pltpu.make_async_remote_copy(
            src_ref=obuf.at[g, t],
            dst_ref=out_ref.at[:, columns(g, h)],
            send_sem=out_send.at[g, i],
            recv_sem=out_recv.at[g, i],
            device_id={"seq": b, "head": t},
            device_id_type=MESH,
        )

    def receive(g, i):
        source = source_at(i)
        return pltpu.make_async_remote_copy(
            src_ref=obuf.at[g, 0],
            dst_ref=out_ref.at[:, columns(g, source)],
            send_sem=out_send.at[g, i],
            recv_sem=out_recv.at[g, i],
            device_id={"seq": b, "head": source},
            device_id_type=MESH,
        )

    def keep(g):
        return pltpu.make_async_copy(
            obuf.at[g, h], out_ref.at[:, columns(g, h)], own_sem.at[g]
        )

    below = lax.broadcasted_iota(jnp.int32, (tile, tile), 1) <= lax.broadcasted_iota(
        jnp.int32, (tile, tile), 0
    )
    rows_all = GROUP * tile

    def scores_of(g, t, start, size):
        rows = pl.ds(pl.multiple_of(t * tile, tile), tile)
        keys = pl.ds(pl.multiple_of(start, tile), size)
        marks = qdoc[rows, :]
        query_ext = jnp.concatenate([
            jnp.concatenate([qbuf[rows, column:column + HD], marks], 1)
            for column in ((g * GROUP + m) * HD for m in range(GROUP))
        ], 0)
        key_ext = jnp.concatenate([kbuf[g, keys, :], kdoc[keys, :]], 1)
        return lax.dot_general(
            query_ext, key_ext, (((1,), (1,)), ((), ())), preferred_element_type=jnp.float32
        )

    def weigh_near(g, t):
        scores = scores_of(g, t, t * tile + far, near)
        edge = jnp.where(jnp.concatenate([below] * GROUP, 0), scores[:, near - tile:], FAR)
        scores = jnp.concatenate([scores[:, :near - tile], edge], 1)
        largest = jnp.max(scores, axis=1, keepdims=True)
        near_w[g, t] = jnp.exp2((scores - largest) * EXP2_SCALE).astype(jnp.bfloat16)
        peak[g, t] = jnp.broadcast_to(largest, (rows_all, HD))

    def weigh_far(g, t):
        scores = scores_of(g, t, t * tile, far)
        before = peak[g, t]
        largest = jnp.maximum(jnp.max(scores, axis=1, keepdims=True), before)
        fade[g, t] = jnp.exp2((before - largest) * EXP2_SCALE)
        far_w[g, t] = jnp.exp2(
            (scores - jnp.concatenate([largest] * (far // HD), 1)) * EXP2_SCALE
        ).astype(jnp.bfloat16)

    def values_of(g, start, size):
        keys = pl.ds(pl.multiple_of(start, tile), size)
        return jnp.concatenate([vbuf[g, keys, :], jnp.ones((size, HD), jnp.bfloat16)], 1)

    def blend(g, t):
        near_v = values_of(g, t * tile + far, near)
        far_v = values_of(g, t * tile, far)
        for part in range(GROUP // PAIR):
            rows = slice(part * PAIR * tile, (part + 1) * PAIR * tile)
            faded = fade[g, t, rows, :]
            mixed = jnp.dot(near_w[g, t, rows, :], near_v, preferred_element_type=jnp.float32)
            mixed = mixed * jnp.concatenate([faded, faded], 1) + jnp.dot(
                far_w[g, t, rows, :], far_v, preferred_element_type=jnp.float32
            )
            result = (mixed[:, :HD] / mixed[:, HD:]).astype(jnp.bfloat16)
            for m in range(PAIR):
                column = (part * PAIR + m) * HD
                obuf[g, t, :, column:column + HD] = result[m * tile:(m + 1) * tile]

    for parity, _, events in starts:
        @pl.when(parity)
        def _():
            for kind, a, pieces in events:
                relay(kind, 0, a, pieces)

    for g in range(groups):
        later = g + 1 < groups
        wait_for(even, 1, g, K, LOW[K])
        wait_for(odd, 2, g, K, HIGH[K])

        def near_step(i, _):
            if later:
                weigh_near(g, tile_at(i))
            else:
                @pl.when(i < n_head // 2)
                def _():
                    weigh_near(g, tile_at(i))
            follow("near", i, g)
            return 0

        lax.fori_loop(0, n_head, near_step, 0)
        wait_for(even, 0, g, K, ALL)
        wait_for(odd, 0, g, K, HIGH[K])

        def far_step(j, _):
            if later:
                for m in range(2):
                    weigh_far(g, tile_at(2 * j + m))
            else:
                @pl.when(j < n_head // 4)
                def _():
                    for m in range(2):
                        weigh_far(g, tile_at(2 * j + m))
            follow("far", 2 * j + 1, g)
            return 0

        lax.fori_loop(0, n_head // 2, far_step, 0)
        wait_for(even, 1, g, V, LOW[V])
        wait_for(odd, 2, g, V, HIGH[V])
        wait_for(even, 0, g, V, ALL)
        wait_for(even, 2, g, V, DIAG[V])
        wait_for(odd, 0, g, V, HIGH[V])

        def blend_far(i, _):
            t = tile_at(i)
            blend(g, t)
            deliver(g, i, t).start()
            follow("blend", i, g)
            return 0

        lax.fori_loop(0, n_head // 2, blend_far, 0)

    for g in range(groups):
        def blend_near(i, _):
            t = tile_at(i)
            if g + 1 == groups:
                weigh_near(g, t)
                weigh_far(g, t)
            blend(g, t)

            @pl.when(i < n_head - 1)
            def _():
                deliver(g, i, t).start()

            @pl.when(i == n_head - 1)
            def _():
                keep(g).start()
            return 0

        lax.fori_loop(n_head // 2, n_head, blend_near, 0)

    for kind, (condition, pieces, *_) in routes.items():
        @pl.when(condition)
        def _():
            for g in range(groups):
                for a in (K, V):
                    for p in pieces[a]:
                        route(kind, g, a, p)[1].wait_send()
    for g in range(groups):
        keep(g).wait()
        for i in range(n_head - 1):
            deliver(g, i, tile_at(i)).wait_send()
            receive(g, i).wait_recv()


def per_device(n_seq, n_head, queries, key_rows, value_rows, doc_lengths):
    tokens = queries.shape[0]
    groups = key_rows.shape[1] // HD
    tile = tokens // n_head
    window = SPAN * tokens
    flops = 4 * tokens * (GROUP * groups) * window * HD
    return pl.pallas_call(
        functools.partial(kernel, n_seq, n_head),
        out_shape=pltpu.VMEM((tile, H * HD), jnp.bfloat16),
        in_specs=[pl.BlockSpec(memory_space=pl.ANY)] * 4,
        out_specs=pl.BlockSpec(memory_space=pl.ANY),
        scratch_shapes=[
            pltpu.VMEM((tokens, GROUP * groups * HD), jnp.bfloat16),
            pltpu.VMEM((groups, window, HD), jnp.bfloat16),
            pltpu.VMEM((groups, window, HD), jnp.bfloat16),
            pltpu.VMEM((tokens, HD), jnp.bfloat16),
            pltpu.VMEM((window, HD), jnp.bfloat16),
            pltpu.VMEM((groups, n_head, GROUP * tile, tokens * (SPAN - 2) + tile), jnp.bfloat16),
            pltpu.VMEM((groups, n_head, GROUP * tile, tokens), jnp.bfloat16),
            pltpu.VMEM((groups, n_head, GROUP * tile, HD), jnp.float32),
            pltpu.VMEM((groups, n_head, GROUP * tile, HD), jnp.float32),
            pltpu.VMEM((groups, n_head, tile, GROUP * HD), jnp.bfloat16),
            pltpu.SemaphoreType.DMA((groups + 1, 2)),
            pltpu.SemaphoreType.DMA((5, groups, 2, PIECES)),
            pltpu.SemaphoreType.DMA((SPAN - 1, groups, 2, PIECES)),
            pltpu.SemaphoreType.DMA((groups, n_head - 1)),
            pltpu.SemaphoreType.DMA((groups, n_head - 1)),
            pltpu.SemaphoreType.DMA((groups,)),
            pltpu.SMEM(doc_lengths.shape, jnp.int32),
            pltpu.SemaphoreType.DMA,
        ],
        compiler_params=pltpu.CompilerParams(
            collective_id=0, has_side_effects=True, vmem_limit_bytes=56 << 20
        ),
        cost_estimate=pl.CostEstimate(flops=flops, bytes_accessed=4 << 20, transcendentals=0),
    )(doc_lengths, queries, key_rows, value_rows)


def solution(mesh):
    body = functools.partial(per_device, mesh.shape["seq"], mesh.shape["head"])
    in_specs = (P("seq", "head"), P("seq", "head"), P("seq", "head"), P())
    out_specs = P(("seq", "head"), None)
    return jax.shard_map(body, mesh=mesh, in_specs=in_specs, out_specs=out_specs, check_vma=False)
```
